32 devices in a mesh: dp: 4 (over y, x), seq: 8 (over z, core).
Axes of the slice: x: 2, y: 2, z: 4, core: 2. Of those that a mesh axis runs over, the one named last changes fastest.
Arguments:
- tokens: bfloat16 [4, 2048, 1024], P('dp', 'seq'), may hold values from -6 to 6
- segment_ids: int32 [4, 2048], P('dp'), may hold values from 0 to 7, never falling along the last dimension, each value on 1 to 1024 neighbouring positions
- w_query: bfloat16 [1024, 1024], P(('dp', 'seq')), may hold values from -0.1875 to 0.1875
- w_key: bfloat16 [1024, 512], P(('dp', 'seq')), may hold values from -0.1875 to 0.1875
- w_value: bfloat16 [1024, 512], P(('dp', 'seq')), may hold values from -0.1875 to 0.1875
- w_out: bfloat16 [1024, 1024], P(('dp', 'seq')), may hold values from -1.5 to 1.5
- attn_gain: bfloat16 [1024], P(('dp', 'seq')), may hold values from 0.5 to 1.5
- query_gain: bfloat16 [64], replicated, may hold values from 0.25 to 1.75
- key_gain: bfloat16 [64], replicated, may hold values from 0.25 to 1.75
- w_gate: bfloat16 [1024, 4608], P(('dp', 'seq')), may hold values from -0.1875 to 0.1875
- w_up: bfloat16 [1024, 4608], P(('dp', 'seq')), may hold values from -0.1875 to 0.1875
- w_down: bfloat16 [4608, 1024], P(('dp', 'seq')), may hold values from -0.09375 to 0.09375
- ffn_gain: bfloat16 [1024], P(('dp', 'seq')), may hold values from 0.5 to 1.5
- cotangent: bfloat16 [4, 2048, 1024], P('dp', 'seq'), may hold values from -6 to 6
Outputs:
- output: bfloat16 [4, 2048, 1024], P('dp', 'seq')
- d_tokens: float32 [4, 2048, 1024], P('dp', 'seq')
- d_w_query: float32 [1024, 1024], P(('dp', 'seq'))
- d_w_key: float32 [1024, 512], P(('dp', 'seq'))
- d_w_value: float32 [1024, 512], P(('dp', 'seq'))
- d_w_out: float32 [1024, 1024], P(('dp', 'seq'))
- d_attn_gain: float32 [1024], P(('dp', 'seq'))
- d_query_gain: float32 [64], replicated
- d_key_gain: float32 [64], replicated
- d_w_gate: float32 [1024, 4608], P(('dp', 'seq'))
- d_w_up: float32 [1024, 4608], P(('dp', 'seq'))
- d_w_down: float32 [4608, 1024], P(('dp', 'seq'))
- d_ffn_gain: float32 [1024], P(('dp', 'seq'))
The draws below stay inside these ranges and needn't reach their ends.
Inputs may be any that keep to these rules, and one draw needn't show every extreme that they name: `segment_ids`: within a sequence the ids never fall; every document holds 1 to 1024 positions, and some document holds exactly 1024.
All inputs are finite; a program needn't handle non-finite values.
Results may differ from the reference program's by a relative error of at most 0.015.
Values may be sent and summed in bfloat16 or wider, within the bound.
No kernel may reach another device: no remote copies, remote signals or barrier semaphores. Data moves between devices by JAX's collectives and lax.ppermute only.
A program may use at most 192 MiB of HBM per device.

```python
import math
import jax
import jax.numpy as jnp
import numpy as np
from jax import lax

D = 1024
H = 16
KVH = 8
HD = 64
FF = 4608
LEN = 2048
NSEQ = 4


def block_levels(rng, extent, shards, smallest, high):
    gain, own = 1.0, jax.random.fold_in(rng, 6)
    for position, blocks in shards:
        heights = jnp.exp(jax.random.uniform(jax.random.fold_in(own, position), (blocks,), jnp.float32, smallest / len(shards), high / len(shards)))
        gain = gain * jnp.repeat(heights, extent[position] // blocks).reshape([-1 if axis == position else 1 for axis in range(len(extent))])
    return gain


def length_profile(number_of, total, limit, skew):
    portions = [(1 << 20) // math.isqrt(standing ** skew) + 1 for standing in range(2, number_of + 1)]
    rest, holding = total - limit - (number_of - 1), [1] * (number_of - 1)
    while rest > 0:
        candidates = [i for i in range(number_of - 1) if holding[i] < limit]
        mass, left = sum([portions[i] for i in candidates]), rest
        for i in candidates:
            extra = min(limit - holding[i], max(1, left * portions[i] // mass), rest)
            holding[i] = holding[i] + extra
            rest = rest - extra
    return np.array([limit] + holding)


def uneven(stream_key, count, total, reach, skew):
    if count == 2:
        one = jax.random.randint(stream_key, (), max(1, total - reach), min(reach, total - 1) + 1)
        return jnp.stack([one, total - one])
    tallies = jnp.asarray(length_profile(count, total, reach, skew), jnp.int32)
    couples = (count - 1) // 2
    giver, taker = tallies[1:1 + 2 * couples:2], tallies[2:2 + 2 * couples:2]
    slack = jnp.minimum(giver - 1, reach - taker)
    moved = jax.random.randint(jax.random.fold_in(stream_key, 1), (couples,), 0, 1 << 20) % (slack + 1)
    tallies = tallies.at[1:1 + 2 * couples:2].set(giver - moved).at[2:2 + 2 * couples:2].set(taker + moved)
    return tallies[jax.random.permutation(jax.random.fold_in(stream_key, 2), count)]


def gaussian(stream_key, dims, width, reach, shards=(), kind=jnp.bfloat16):
    drawn = jax.random.normal(stream_key, dims, jnp.float32) * width
    if len(shards) > 0:
        drawn = block_levels(stream_key, dims, shards, -0.22, 0.18) * drawn
    return jnp.clip(drawn, min=-reach, max=reach).astype(kind)


def setup_inputs(seed: int = 0) -> dict:
    key_of = jax.random.split(jax.random.key(seed), 15)
    return {
        "tokens": gaussian(key_of[0], (NSEQ, LEN, D), 1.0, 6.0, ((0, 4), (1, 8))),
        "segment_ids": jax.vmap(lambda own: jnp.searchsorted(jnp.cumsum(uneven(own, 8, LEN, LEN // 2, 1)), jnp.arange(LEN), side="right"))(jax.random.split(key_of[1], NSEQ)).reshape((NSEQ, LEN)).astype(jnp.int32),
        "w_query": gaussian(key_of[2], (D, H * HD), D ** -0.5, 0.1875, ((0, 32),)),
        "w_key": gaussian(key_of[3], (D, KVH * HD), D ** -0.5, 0.1875, ((0, 32),)),
        "w_value": gaussian(key_of[4], (D, KVH * HD), D ** -0.5, 0.1875, ((0, 32),)),
        "w_out": gaussian(key_of[5], (H * HD, D), (H * HD // 64) ** -0.5, 1.5, ((0, 32),)),
        "attn_gain": jnp.clip(1.0 + 0.1 * jax.random.normal(key_of[6], (D,), jnp.float32), 0.5, 1.5).astype(jnp.bfloat16),
        "query_gain": jnp.clip(1.0 + 0.15 * jax.random.normal(key_of[7], (HD,), jnp.float32), 0.25, 1.75).astype(jnp.bfloat16),
        "key_gain": jnp.clip(1.0 + 0.15 * jax.random.normal(key_of[8], (HD,), jnp.float32), 0.25, 1.75).astype(jnp.bfloat16),
        "w_gate": gaussian(key_of[9], (D, FF), D ** -0.5, 0.1875, ((0, 32),)),
        "w_up": gaussian(key_of[10], (D, FF), D ** -0.5, 0.1875, ((0, 32),)),
        "w_down": gaussian(key_of[11], (FF, D), FF ** -0.5, 0.09375, ((0, 32),)),
        "ffn_gain": jnp.clip(1.0 + 0.1 * jax.random.normal(key_of[12], (D,), jnp.float32), 0.5, 1.5).astype(jnp.bfloat16),
        "cotangent": gaussian(key_of[13], (NSEQ, LEN, D), 1.0, 6.0, ((0, 4), (1, 8))),
    }


EPSILON = 1e-05
ROPE_BASE = 1000000.0

def narrow(values):
    return lax.optimization_barrier(values.astype(jnp.bfloat16))

def rms_scale(values):
    return lax.rsqrt(lax.optimization_barrier(jnp.mean(values * values, axis=-1, keepdims=True)) + EPSILON)

def rope_tables(positions, head_width):
    half_width = head_width // 2
    frequency = ROPE_BASE ** (-(jnp.arange(half_width, dtype=jnp.float32) * 2.0 / head_width))
    angles = positions.astype(jnp.float32)[:, None] * frequency[None, :]
    return (jnp.cos(angles), jnp.sin(angles))

def rotate(values, cosine_table, sine_table):
    half_width = values.shape[-1] // 2
    front_half = values[..., :half_width]
    back_half = values[..., half_width:]
    return jnp.concatenate([front_half * cosine_table - back_half * sine_table, back_half * cosine_table + front_half * sine_table], axis=-1)

def unrotate(incoming, cosine_table, sine_table):
    half_width = incoming.shape[-1] // 2
    front_half = incoming[..., :half_width]
    back_half = incoming[..., half_width:]
    return jnp.concatenate([front_half * cosine_table + back_half * sine_table, back_half * cosine_table - front_half * sine_table], axis=-1)

def norm_back(incoming, values, scale_vec, gain_vector, sum_axes):
    upstream = incoming * gain_vector
    grad_values = scale_vec * (upstream - values * scale_vec * scale_vec * lax.optimization_barrier(jnp.mean(upstream * values, axis=-1, keepdims=True)))
    grad_gain = lax.optimization_barrier(jnp.sum(incoming * values * scale_vec, axis=sum_axes))
    return (grad_values, grad_gain)

def reference(tokens, segment_ids, w_query, w_key, w_value, w_out, attn_gain, query_gain, key_gain, w_gate, w_up, w_down, ffn_gain, cotangent):
    group_size = H // KVH
    softmax_scale = HD ** (-0.5)
    block_len = min(512, LEN)
    block_count = LEN // block_len
    positions = jnp.arange(LEN, dtype=jnp.int32)
    cosine_table, sine_table = rope_tables(positions, HD)
    cosine_table = cosine_table[:, None, :]
    sine_table = sine_table[:, None, :]
    gain_attn = attn_gain.astype(jnp.float32)
    gain_query = query_gain.astype(jnp.float32)
    gain_key = key_gain.astype(jnp.float32)
    gain_ffn = ffn_gain.astype(jnp.float32)
    block_ids = jnp.arange(block_count, dtype=jnp.int32)

    def one_sequence(grad_sums, inputs):
        seq_tokens, seq_ids, seq_cotangent = inputs
        stream = seq_tokens.astype(jnp.float32)
        scale_one = rms_scale(stream)
        normed_one = narrow(stream * scale_one * gain_attn)
        query_pre = jnp.dot(normed_one, w_query, preferred_element_type=jnp.float32).reshape(LEN, H, HD)
        key_pre = jnp.dot(normed_one, w_key, preferred_element_type=jnp.float32).reshape(LEN, KVH, HD)
        value_pre = jnp.dot(normed_one, w_value, preferred_element_type=jnp.float32)
        query_scale = rms_scale(query_pre)
        key_scale = rms_scale(key_pre)
        query_rot = narrow(rotate(query_pre * query_scale * gain_query, cosine_table, sine_table))
        key_rot = narrow(rotate(key_pre * key_scale * gain_key, cosine_table, sine_table))
        value_bf = narrow(value_pre)
        query_wide = query_rot.astype(jnp.float32).reshape(LEN, KVH, group_size, HD)
        keys_wide = key_rot.astype(jnp.float32)
        values_wide = value_bf.astype(jnp.float32).reshape(LEN, KVH, HD)

        def scores_of(block_num):
            offset = block_num * block_len
            query_block = lax.dynamic_slice_in_dim(query_wide, offset, block_len, 0)
            query_pos = lax.dynamic_slice_in_dim(positions, offset, block_len, 0)
            query_ids = lax.dynamic_slice_in_dim(seq_ids, offset, block_len, 0)
            allowed = (positions[None, :] <= query_pos[:, None]) & (seq_ids[None, :] == query_ids[:, None])
            scores = jnp.einsum('qgrd,kgd->grqk', query_block, keys_wide) * softmax_scale
            return (query_block, allowed, scores)

        def forward_block(block_num):
            query_block, allowed, scores = scores_of(block_num)
            weights = jnp.where(allowed, jnp.exp(scores), 0.0)
            denominator = lax.optimization_barrier(jnp.sum(weights, axis=-1))
            summed = jnp.einsum('grqk,kgd->qgrd', narrow(weights).astype(jnp.float32), values_wide)
            attended_block = narrow(summed / jnp.transpose(denominator, (2, 0, 1))[..., None])
            return (attended_block, jnp.log(denominator))
        attended, log_total = lax.map(forward_block, block_ids)
        attended = attended.reshape(LEN, H * HD)
        log_total = jnp.transpose(log_total, (1, 2, 0, 3)).reshape(KVH, group_size, LEN)
        middle = stream + jnp.dot(attended, w_out, preferred_element_type=jnp.float32)
        scale_two = rms_scale(middle)
        normed_two = narrow(middle * scale_two * gain_ffn)
        gate_pre = jnp.dot(normed_two, w_gate, preferred_element_type=jnp.float32)
        up_pre = jnp.dot(normed_two, w_up, preferred_element_type=jnp.float32)
        sigmoid_gate = jax.nn.sigmoid(gate_pre)
        silu_gate = gate_pre * sigmoid_gate
        hidden = narrow(silu_gate * up_pre)
        output = (middle + jnp.dot(hidden, w_down, preferred_element_type=jnp.float32)).astype(jnp.bfloat16)
        grad_output = seq_cotangent.astype(jnp.float32)
        grad_hidden = jnp.dot(seq_cotangent, w_down.T, preferred_element_type=jnp.float32)
        grad_down_w = jnp.dot(hidden.T, seq_cotangent, preferred_element_type=jnp.float32)
        grad_gate = narrow(grad_hidden * up_pre * sigmoid_gate * (1.0 + gate_pre * (1.0 - sigmoid_gate)))
        grad_up = narrow(grad_hidden * silu_gate)
        grad_gate_w = jnp.dot(normed_two.T, grad_gate, preferred_element_type=jnp.float32)
        grad_up_w = jnp.dot(normed_two.T, grad_up, preferred_element_type=jnp.float32)
        grad_normed_two = jnp.dot(grad_gate, w_gate.T, preferred_element_type=jnp.float32) + jnp.dot(grad_up, w_up.T, preferred_element_type=jnp.float32)
        grad_mid_norm, grad_ffn_gain = norm_back(grad_normed_two, middle, scale_two, gain_ffn, (0,))
        grad_middle = grad_output + grad_mid_norm
        grad_middle_bf = narrow(grad_middle)
        grad_out_w = jnp.dot(attended.T, grad_middle_bf, preferred_element_type=jnp.float32)
        grad_attended = narrow(jnp.dot(grad_middle_bf, w_out.T, preferred_element_type=jnp.float32))
        grad_att_wide = grad_attended.astype(jnp.float32).reshape(LEN, KVH, group_size, HD)
        attended_wide = attended.astype(jnp.float32).reshape(LEN, KVH, group_size, HD)
        delta_rows = jnp.transpose(lax.optimization_barrier(jnp.sum(grad_att_wide * attended_wide, axis=-1)), (1, 2, 0))

        def backward_block(running, block_num):
            grad_keys, grad_values = running
            offset = block_num * block_len
            query_block, allowed, scores = scores_of(block_num)
            total_block = lax.dynamic_slice_in_dim(log_total, offset, block_len, 2)
            delta_block = lax.dynamic_slice_in_dim(delta_rows, offset, block_len, 2)
            incoming_block = lax.dynamic_slice_in_dim(grad_att_wide, offset, block_len, 0)
            probabilities = jnp.where(allowed, jnp.exp(scores - total_block[..., None]), 0.0)
            grad_probs = jnp.einsum('qgrd,kgd->grqk', incoming_block, values_wide)
            grad_scores = narrow(probabilities * (grad_probs - delta_block[..., None])).astype(jnp.float32)
            grad_values = grad_values + jnp.einsum('grqk,qgrd->kgd', narrow(probabilities).astype(jnp.float32), incoming_block)
            grad_keys = grad_keys + jnp.einsum('grqk,qgrd->kgd', grad_scores, query_block) * softmax_scale
            grad_query = jnp.einsum('grqk,kgd->qgrd', grad_scores, keys_wide) * softmax_scale
            return ((grad_keys, grad_values), grad_query)
        zero_keys = jnp.zeros((LEN, KVH, HD), jnp.float32)
        (grad_keys, grad_values), grad_query = lax.scan(backward_block, (zero_keys, zero_keys), block_ids)
        grad_query = grad_query.reshape(LEN, H, HD)
        grad_qnorm = unrotate(grad_query, cosine_table, sine_table)
        grad_qpre, grad_qgain = norm_back(grad_qnorm, query_pre, query_scale, gain_query, (0, 1))
        grad_knorm = unrotate(grad_keys, cosine_table, sine_table)
        grad_kpre, grad_kgain = norm_back(grad_knorm, key_pre, key_scale, gain_key, (0, 1))
        query_bf = narrow(grad_qpre.reshape(LEN, H * HD))
        key_bf = narrow(grad_kpre.reshape(LEN, KVH * HD))
        value_grad_bf = narrow(grad_values.reshape(LEN, KVH * HD))
        grad_query_w = jnp.dot(normed_one.T, query_bf, preferred_element_type=jnp.float32)
        grad_key_w = jnp.dot(normed_one.T, key_bf, preferred_element_type=jnp.float32)
        grad_value_w = jnp.dot(normed_one.T, value_grad_bf, preferred_element_type=jnp.float32)
        grad_normed_one = jnp.dot(query_bf, w_query.T, preferred_element_type=jnp.float32) + jnp.dot(key_bf, w_key.T, preferred_element_type=jnp.float32) + jnp.dot(value_grad_bf, w_value.T, preferred_element_type=jnp.float32)
        grad_stream, grad_attn_gain = norm_back(grad_normed_one, stream, scale_one, gain_attn, (0,))
        grad_tokens = grad_middle + grad_stream
        terms = (grad_query_w, grad_key_w, grad_value_w, grad_out_w, grad_attn_gain, grad_qgain, grad_kgain, grad_gate_w, grad_up_w, grad_down_w, grad_ffn_gain)
        updated = tuple((left + right for left, right in zip(grad_sums, terms)))
        return (updated, (output, grad_tokens))
    start_sums = (jnp.zeros((D, H * HD), jnp.float32), jnp.zeros((D, KVH * HD), jnp.float32), jnp.zeros((D, KVH * HD), jnp.float32), jnp.zeros((H * HD, D), jnp.float32), jnp.zeros((D,), jnp.float32), jnp.zeros((HD,), jnp.float32), jnp.zeros((HD,), jnp.float32), jnp.zeros((D, FF), jnp.float32), jnp.zeros((D, FF), jnp.float32), jnp.zeros((FF, D), jnp.float32), jnp.zeros((D,), jnp.float32))
    grad_sums, (outputs, grad_inputs) = lax.scan(one_sequence, start_sums, (tokens, segment_ids, cotangent))
    return (outputs, grad_inputs, grad_sums[0], grad_sums[1], grad_sums[2], grad_sums[3], grad_sums[4], grad_sums[5], grad_sums[6], grad_sums[7], grad_sums[8], grad_sums[9], grad_sums[10])
```

```python
import jax
import jax.numpy as jnp
from jax import lax
from jax.sharding import PartitionSpec as P

EPSILON = 1e-05
ROPE_BASE = 1000000.0
F32 = jnp.float32
BF16 = jnp.bfloat16
BOTH = ("dp", "seq")


def rms_scale(values):
    return lax.rsqrt(jnp.mean(values * values, axis=-1, keepdims=True) + EPSILON)


def rope_tables(positions, head_width):
    half_width = head_width // 2
    frequency = ROPE_BASE ** (-(jnp.arange(half_width, dtype=F32) * 2.0 / head_width))
    angles = positions.astype(F32)[:, None] * frequency[None, :]
    return (jnp.cos(angles), jnp.sin(angles))


def rotate(values, cosine_table, sine_table):
    half_width = values.shape[-1] // 2
    front_half = values[..., :half_width]
    back_half = values[..., half_width:]
    return jnp.concatenate(
        [
            front_half * cosine_table - back_half * sine_table,
            back_half * cosine_table + front_half * sine_table,
        ],
        axis=-1,
    )


def unrotate(incoming, cosine_table, sine_table):
    return rotate(incoming, cosine_table, -sine_table)


def norm_back(incoming, values, scale_vec, gain_vector, sum_axes):
    upstream = incoming * gain_vector
    grad_values = scale_vec * (
        upstream
        - values * scale_vec * scale_vec * jnp.mean(upstream * values, axis=-1, keepdims=True)
    )
    grad_gain = jnp.sum(incoming * values * scale_vec, axis=sum_axes)
    return (grad_values, grad_gain)


def dot(left, right):
    return jnp.dot(left, right, preferred_element_type=F32)


def dot_tn(left, right):
    return lax.dot_general(left, right, (((0,), (0,)), ((), ())), preferred_element_type=F32)


def dot_nt(left, right):
    return lax.dot_general(left, right, (((1,), (1,)), ((), ())), preferred_element_type=F32)


def swap_dp(value, bits, count):
    return lax.ppermute(value, "dp", [(i, i ^ bits) for i in range(count)])


def gather_dp(value, count):
    if count != 4:
        return lax.all_gather(value, "dp", axis=0, tiled=True)
    half = value.shape[0] // 2
    one = swap_dp(value, 1, count)
    two = swap_dp(value, 2, count)
    top = swap_dp(two[:half], 1, count)
    bottom = swap_dp(one[half:], 2, count)
    return jnp.concatenate([value, one, two, top, bottom], axis=0)


def scatter_sum_dp(parts, count):
    if count != 4:
        return lax.psum_scatter(parts, "dp", scatter_dimension=0, tiled=True).astype(F32)
    rows = parts.shape[0] // 4
    half = rows // 2
    own, one, two, far = (parts[i * rows : (i + 1) * rows] for i in range(4))
    top = swap_dp(far[:half], 1, count).astype(F32)
    bottom = swap_dp(far[half:], 2, count).astype(F32)
    two_sum = jnp.concatenate(
        [(two[:half].astype(F32) + top).astype(BF16), two[half:]], axis=0
    )
    one_sum = jnp.concatenate(
        [one[:half], (one[half:].astype(F32) + bottom).astype(BF16)], axis=0
    )
    from_one = swap_dp(one_sum, 1, count).astype(F32)
    from_two = swap_dp(two_sum, 2, count).astype(F32)
    return own.astype(F32) + from_one + from_two


def make_body(dp_count, seq_shards):
    def shift_seq(value, step):
        pairs = [(i, i + step) for i in range(seq_shards) if 0 <= i + step < seq_shards]
        return lax.ppermute(value, "seq", pairs)

    def swap_core(value):
        return lax.ppermute(value, "seq", [(i, i ^ 1) for i in range(seq_shards)])

    def body(
        tokens,
        segment_ids,
        w_query,
        w_key,
        w_value,
        w_out,
        attn_gain,
        query_gain,
        key_gain,
        w_gate,
        w_up,
        w_down,
        ffn_gain,
        cotangent,
    ):
        _, local_len, model_width = tokens.shape
        seq_len = segment_ids.shape[1]
        head_width = query_gain.shape[0]
        query_width = w_query.shape[1]
        key_width = w_key.shape[1]
        query_heads = query_width // head_width
        key_heads = key_width // head_width
        group_size = query_heads // key_heads
        softmax_scale = head_width ** (-0.5)
        rows = w_query.shape[0]
        ffn_width = w_gate.shape[1]
        ffn_part = ffn_width // dp_count
        seq_rank = lax.axis_index("seq")
        core = seq_rank % 2
        first_row = seq_rank * local_len
        tokens = tokens[0]
        cotangent = cotangent[0]
        ids = segment_ids[0]

        reach = -(-(seq_len // 2 - 1) // local_len)
        hops = -(-reach // 2)

        gains = jnp.stack([attn_gain, ffn_gain], axis=1)
        gains = jnp.pad(gains, ((0, 0), (0, 126)))
        pack = jnp.concatenate([w_query, w_key, w_value, gains], axis=1)
        pack = lax.all_gather(pack, BOTH, axis=0, tiled=True)
        qkv_all = pack[:, : query_width + 2 * key_width]
        gain_cols = pack[:, query_width + 2 * key_width :].astype(F32)
        attn_gain_all = gain_cols[:, 0]
        ffn_gain_all = gain_cols[:, 1]
        out_all = lax.all_gather(w_out, BOTH, axis=0, tiled=True)

        gate_up = jnp.concatenate(
            [
                w_gate.reshape(rows, dp_count, ffn_part),
                w_up.reshape(rows, dp_count, ffn_part),
            ],
            axis=2,
        )
        gate_up = lax.all_to_all(jnp.moveaxis(gate_up, 1, 0), "dp", 0, 0, tiled=True)
        down_all = lax.all_gather(w_down, "seq", axis=0, tiled=True)
        gate_up_all = lax.all_gather(gate_up, "seq", axis=1, tiled=True).reshape(
            model_width, 2 * ffn_part
        )
        cotangent_all = gather_dp(cotangent, dp_count)

        stream = tokens.astype(F32)
        scale_one = rms_scale(stream)
        normed_one = (stream * scale_one * attn_gain_all).astype(BF16)
        positions = first_row + jnp.arange(local_len, dtype=jnp.int32)
        cosine_table, sine_table = rope_tables(positions, head_width)
        cosine_table = cosine_table[:, None, :]
        sine_table = sine_table[:, None, :]
        qkv = dot(normed_one, qkv_all)
        query_pre = qkv[:, :query_width].reshape(local_len, query_heads, head_width)
        key_pre = qkv[:, query_width : query_width + key_width].reshape(
            local_len, key_heads, head_width
        )
        value_send = qkv[:, query_width + key_width :].astype(BF16)
        query_scale = rms_scale(query_pre)
        key_scale = rms_scale(key_pre)
        query_gain_f = query_gain.astype(F32)
        key_gain_f = key_gain.astype(F32)
        query_rot = rotate(
            query_pre * query_scale * query_gain_f, cosine_table, sine_table
        ).astype(BF16)
        key_rot = (
            rotate(key_pre * key_scale * key_gain_f, cosine_table, sine_table)
            .astype(BF16)
            .reshape(local_len, key_width)
        )

        both = [jnp.concatenate([key_rot, value_send], axis=1)]
        for _ in range(hops):
            both.append(shift_seq(both[-1], 2))
        for_even = jnp.concatenate(both[:-1], axis=0)
        for_odd = jnp.concatenate(both[1:], axis=0)
        across = swap_core(jnp.where(core == 0, for_even, for_odd))
        window = jnp.concatenate(both + [across], axis=0)
        block_steps = [-2 * i for i in range(hops + 1)] + [-1 - 2 * i for i in range(hops)]
        starts = [first_row + step * local_len for step in block_steps]
        key_pos = jnp.concatenate([start + jnp.arange(local_len, dtype=jnp.int32) for start in starts])
        key_ids = jnp.concatenate(
            [
                lax.dynamic_slice_in_dim(ids, jnp.maximum(start, 0), local_len, 0)
                for start in starts
            ]
        )
        query_ids = lax.dynamic_slice_in_dim(ids, first_row, local_len, 0)
        allowed = (
            (key_pos[None, :] <= positions[:, None])
            & (key_pos[None, :] >= 0)
            & (key_ids[None, :] == query_ids[:, None])
        )[None, None]
        window_len = window.shape[0]
        keys = window[:, :key_width].reshape(window_len, key_heads, head_width)
        values = window[:, key_width:].reshape(window_len, key_heads, head_width)
        queries = query_rot.reshape(local_len, key_heads, group_size, head_width)
        scores = (
            jnp.einsum("qgrd,kgd->grqk", queries, keys, preferred_element_type=F32)
            * softmax_scale
        )
        weights = jnp.where(allowed, jnp.exp(scores), 0.0)
        denominator = jnp.sum(weights, axis=-1)
        summed = jnp.einsum(
            "grqk,kgd->qgrd", weights.astype(BF16), values, preferred_element_type=F32
        )
        attended = (summed / jnp.moveaxis(denominator, 2, 0)[..., None]).astype(BF16)
        log_total = jnp.log(denominator)
        attended_flat = attended.reshape(local_len, query_width)
        middle = stream + dot(attended_flat, out_all)

        scale_two = rms_scale(middle)
        normed_two = (middle * scale_two * ffn_gain_all).astype(BF16)
        normed_all = gather_dp(normed_two, dp_count)
        both_pre = dot(normed_all, gate_up_all)
        gate_pre = both_pre[:, :ffn_part]
        up_pre = both_pre[:, ffn_part:]
        sigmoid_gate = jax.nn.sigmoid(gate_pre)
        silu_gate = gate_pre * sigmoid_gate
        hidden = (silu_gate * up_pre).astype(BF16)
        out_part = dot(hidden, down_all).astype(BF16)
        output = (middle + scatter_sum_dp(out_part, dp_count)).astype(BF16)
        grad_output = cotangent.astype(F32)
        grad_hidden = dot_nt(cotangent_all, down_all)
        grad_gate = (
            grad_hidden * up_pre * sigmoid_gate * (1.0 + gate_pre * (1.0 - sigmoid_gate))
        ).astype(BF16)
        grad_up = (grad_hidden * silu_gate).astype(BF16)
        grad_both = jnp.concatenate([grad_gate, grad_up], axis=1)
        grad_normed_two = scatter_sum_dp(dot_nt(grad_both, gate_up_all).astype(BF16), dp_count)
        grad_down_w = lax.psum_scatter(
            dot_tn(hidden, cotangent_all).astype(BF16), "seq", scatter_dimension=0, tiled=True
        )
        grad_gate_up = lax.psum_scatter(
            dot_tn(normed_all, grad_both)
            .astype(BF16)
            .reshape(dp_count, seq_shards * rows, 2 * ffn_part),
            "seq",
            scatter_dimension=1,
            tiled=True,
        )
        grad_gate_up = lax.all_to_all(grad_gate_up, "dp", 0, 0, tiled=True).astype(F32)
        grad_gate_up = jnp.moveaxis(grad_gate_up, 0, 1)
        grad_gate_w = grad_gate_up[..., :ffn_part].reshape(rows, ffn_width)
        grad_up_w = grad_gate_up[..., ffn_part:].reshape(rows, ffn_width)

        grad_mid_norm, grad_ffn_gain = norm_back(
            grad_normed_two, middle, scale_two, ffn_gain_all, (0,)
        )
        grad_middle = grad_output + grad_mid_norm

        grad_middle_bf = grad_middle.astype(BF16)
        grad_out_w = lax.psum_scatter(
            dot_tn(attended_flat, grad_middle_bf).astype(BF16),
            BOTH,
            scatter_dimension=0,
            tiled=True,
        )
        grad_attended = (
            dot_nt(grad_middle_bf, out_all)
            .astype(BF16)
            .reshape(local_len, key_heads, group_size, head_width)
        )
        delta_rows = jnp.moveaxis(
            jnp.sum(grad_attended.astype(F32) * attended.astype(F32), axis=-1), 0, 2
        )
        probabilities = jnp.where(allowed, jnp.exp(scores - log_total[..., None]), 0.0)
        grad_probs = jnp.einsum(
            "qgrd,kgd->grqk", grad_attended, values, preferred_element_type=F32
        )
        grad_scores = (probabilities * (grad_probs - delta_rows[..., None])).astype(BF16)
        value_term = jnp.einsum(
            "grqk,qgrd->kgd",
            probabilities.astype(BF16),
            grad_attended,
            preferred_element_type=F32,
        )
        key_term = (
            jnp.einsum("grqk,qgrd->kgd", grad_scores, queries, preferred_element_type=F32)
            * softmax_scale
        )
        grad_query = (
            jnp.einsum("grqk,kgd->qgrd", grad_scores, keys, preferred_element_type=F32)
            * softmax_scale
        )
        grad_window = jnp.concatenate(
            [
                key_term.reshape(window_len, key_width),
                value_term.reshape(window_len, key_width),
            ],
            axis=1,
        ).astype(BF16)
        split = (hops + 1) * local_len
        back = swap_core(grad_window[split:])
        zero = jnp.zeros((local_len, 2 * key_width), BF16)
        back = jnp.where(
            core == 0,
            jnp.concatenate([back, zero], axis=0),
            jnp.concatenate([zero, back], axis=0),
        )
        total = grad_window[:split].astype(F32) + back.astype(F32)
        running = total[hops * local_len :]
        for step in range(hops - 1, -1, -1):
            arrived = shift_seq(running.astype(BF16), -2)
            running = total[step * local_len : (step + 1) * local_len] + arrived.astype(F32)
        key_sum = running[:, :key_width]
        value_grad_bf = running[:, key_width:].astype(BF16)
        grad_qnorm = unrotate(
            grad_query.reshape(local_len, query_heads, head_width), cosine_table, sine_table
        )
        grad_qpre, grad_qgain = norm_back(
            grad_qnorm, query_pre, query_scale, query_gain_f, (0, 1)
        )
        grad_knorm = unrotate(
            key_sum.reshape(local_len, key_heads, head_width), cosine_table, sine_table
        )
        grad_kpre, grad_kgain = norm_back(grad_knorm, key_pre, key_scale, key_gain_f, (0, 1))
        grad_qkv = jnp.concatenate(
            [
                grad_qpre.reshape(local_len, query_width).astype(BF16),
                grad_kpre.reshape(local_len, key_width).astype(BF16),
                value_grad_bf,
            ],
            axis=1,
        )
        grad_qkv_w = lax.psum_scatter(
            dot_tn(normed_one, grad_qkv).astype(BF16), BOTH, scatter_dimension=0, tiled=True
        ).astype(F32)
        grad_normed_one = dot_nt(grad_qkv, qkv_all)
        grad_stream, grad_attn_gain = norm_back(
            grad_normed_one, stream, scale_one, attn_gain_all, (0,)
        )
        grad_tokens = grad_middle + grad_stream

        devices = dp_count * seq_shards
        head_gains = jnp.concatenate([grad_qgain, grad_kgain])
        small = jnp.concatenate(
            [
                grad_attn_gain.reshape(devices, rows),
                grad_ffn_gain.reshape(devices, rows),
                jnp.broadcast_to(head_gains, (devices, 2 * head_width)),
            ],
            axis=1,
        )
        small = jnp.sum(lax.all_to_all(small, BOTH, 0, 0, tiled=True), axis=0)
        return (
            output[None],
            grad_tokens[None],
            grad_qkv_w[:, :query_width],
            grad_qkv_w[:, query_width : query_width + key_width],
            grad_qkv_w[:, query_width + key_width :],
            grad_out_w.astype(F32),
            small[:rows],
            small[2 * rows : 2 * rows + head_width],
            small[2 * rows + head_width :],
            grad_gate_w,
            grad_up_w,
            grad_down_w.astype(F32),
            small[rows : 2 * rows],
        )

    return body


def solution(mesh):
    in_specs = (
        P("dp", "seq", None),
        P("dp", None),
        P(BOTH, None),
        P(BOTH, None),
        P(BOTH, None),
        P(BOTH, None),
        P(BOTH),
        P(),
        P(),
        P(BOTH, None),
        P(BOTH, None),
        P(BOTH, None),
        P(BOTH),
        P("dp", "seq", None),
    )
    out_specs = (
        P("dp", "seq", None),
        P("dp", "seq", None),
        P(BOTH, None),
        P(BOTH, None),
        P(BOTH, None),
        P(BOTH, None),
        P(BOTH),
        P(),
        P(),
        P(BOTH, None),
        P(BOTH, None),
        P(BOTH, None),
        P(BOTH),
    )
    body = make_body(mesh.shape["dp"], mesh.shape["seq"])
    return jax.shard_map(body, mesh=mesh, in_specs=in_specs, out_specs=out_specs, check_vma=False)
```

```python
import jax
import jax.numpy as jnp
from jax import lax
from jax.sharding import PartitionSpec as P

EPSILON = 1e-05
ROPE_BASE = 1000000.0
F32 = jnp.float32
BF16 = jnp.bfloat16
BOTH = ("dp", "seq")


def rms_scale(values):
    return lax.rsqrt(jnp.mean(values * values, axis=-1, keepdims=True) + EPSILON)


def rope_tables(positions, head_width):
    half_width = head_width // 2
    frequency = ROPE_BASE ** (-(jnp.arange(half_width, dtype=F32) * 2.0 / head_width))
    angles = positions.astype(F32)[:, None] * frequency[None, :]
    return (jnp.cos(angles), jnp.sin(angles))


def rotate(values, cosine_table, sine_table):
    half_width = values.shape[-1] // 2
    front_half = values[..., :half_width]
    back_half = values[..., half_width:]
    return jnp.concatenate(
        [
            front_half * cosine_table - back_half * sine_table,
            back_half * cosine_table + front_half * sine_table,
        ],
        axis=-1,
    )


def unrotate(incoming, cosine_table, sine_table):
    return rotate(incoming, cosine_table, -sine_table)


def norm_back(incoming, values, scale_vec, gain_vector, sum_axes):
    upstream = incoming * gain_vector
    grad_values = scale_vec * (
        upstream
        - values * scale_vec * scale_vec * jnp.mean(upstream * values, axis=-1, keepdims=True)
    )
    grad_gain = jnp.sum(incoming * values * scale_vec, axis=sum_axes)
    return (grad_values, grad_gain)


def dot(left, right):
    return jnp.dot(left, right, preferred_element_type=F32)


def dot_tn(left, right):
    return lax.dot_general(left, right, (((0,), (0,)), ((), ())), preferred_element_type=F32)


def dot_nt(left, right):
    return lax.dot_general(left, right, (((1,), (1,)), ((), ())), preferred_element_type=F32)


def swap_dp(value, bits, count):
    return lax.ppermute(value, "dp", [(i, i ^ bits) for i in range(count)])


def gather_dp(value, count):
    if count != 4:
        return lax.all_gather(value, "dp", axis=0, tiled=True)
    half = value.shape[0] // 2
    one = swap_dp(value, 1, count)
    two = swap_dp(value, 2, count)
    top = swap_dp(two[:half], 1, count)
    bottom = swap_dp(one[half:], 2, count)
    return jnp.concatenate([value, one, two, top, bottom], axis=0)


def scatter_sum_dp(parts, count):
    if count != 4:
        return lax.psum_scatter(parts, "dp", scatter_dimension=0, tiled=True).astype(F32)
    rows = parts.shape[0] // 4
    half = rows // 2
    own, one, two, far = (parts[i * rows : (i + 1) * rows] for i in range(4))
    top = swap_dp(far[:half], 1, count).astype(F32)
    bottom = swap_dp(far[half:], 2, count).astype(F32)
    two_sum = jnp.concatenate(
        [(two[:half].astype(F32) + top).astype(BF16), two[half:]], axis=0
    )
    one_sum = jnp.concatenate(
        [one[:half], (one[half:].astype(F32) + bottom).astype(BF16)], axis=0
    )
    from_one = swap_dp(one_sum, 1, count).astype(F32)
    from_two = swap_dp(two_sum, 2, count).astype(F32)
    return own.astype(F32) + from_one + from_two


def make_body(dp_count, seq_shards):
    def shift_seq(value, step):
        pairs = [(i, i + step) for i in range(seq_shards) if 0 <= i + step < seq_shards]
        return lax.ppermute(value, "seq", pairs)

    def swap_core(value):
        return lax.ppermute(value, "seq", [(i, i ^ 1) for i in range(seq_shards)])

    def turn_seq(value, step):
        return lax.ppermute(
            value, "seq", [(i, (i + step) % seq_shards) for i in range(seq_shards)]
        )

    pairs = seq_shards // 2
    in_slots = dp_count == 4

    def slot_matrix(width):
        rows = width // (dp_count * seq_shards)
        slot_row = jnp.arange(width, dtype=jnp.int32)
        inner = slot_row % rows
        slot = slot_row // rows
        chip = (lax.axis_index("seq") // 2 + slot % pairs) % pairs
        peer = lax.axis_index("dp") ^ (slot // pairs % dp_count)
        core = (lax.axis_index("seq") % 2) ^ (slot // (pairs * dp_count))
        source = ((peer * seq_shards) + chip * 2 + core) * rows + inner
        return (slot_row[:, None] == source[None, :]).astype(BF16)

    def gather_rows(value):
        if not in_slots:
            return lax.all_gather(value, BOTH, axis=0, tiled=True)
        line = [value] + [turn_seq(value, -2 * k) for k in range(1, pairs)]
        plane = gather_dp(jnp.concatenate(line, axis=0), dp_count)
        return jnp.concatenate([plane, swap_core(plane)], axis=0)

    def scatter_rows(parts):
        if not in_slots:
            return lax.psum_scatter(parts, BOTH, scatter_dimension=0, tiled=True).astype(F32)
        half = parts.shape[0] // 2
        chip = (parts[:half].astype(F32) + swap_core(parts[half:]).astype(F32)).astype(BF16)
        line = scatter_sum_dp(chip, dp_count)
        rows = line.shape[0] // pairs
        total = line[:rows]
        for k in range(1, pairs):
            piece = line[k * rows : (k + 1) * rows].astype(BF16)
            total = total + turn_seq(piece, 2 * k).astype(F32)
        return total

    def body(
        tokens,
        segment_ids,
        w_query,
        w_key,
        w_value,
        w_out,
        attn_gain,
        query_gain,
        key_gain,
        w_gate,
        w_up,
        w_down,
        ffn_gain,
        cotangent,
    ):
        _, local_len, model_width = tokens.shape
        seq_len = segment_ids.shape[1]
        head_width = query_gain.shape[0]
        query_width = w_query.shape[1]
        key_width = w_key.shape[1]
        query_heads = query_width // head_width
        key_heads = key_width // head_width
        group_size = query_heads // key_heads
        softmax_scale = head_width ** (-0.5)
        rows = w_query.shape[0]
        ffn_width = w_gate.shape[1]
        ffn_part = ffn_width // dp_count
        seq_rank = lax.axis_index("seq")
        core = seq_rank % 2
        first_row = seq_rank * local_len
        tokens = tokens[0]
        cotangent = cotangent[0]
        ids = segment_ids[0]

        reach = -(-(seq_len // 2 - 1) // local_len)
        hops = -(-reach // 2)

        gains = jnp.stack([attn_gain, ffn_gain], axis=1)
        gains = jnp.pad(gains, ((0, 0), (0, 126)))
        pack = gather_rows(jnp.concatenate([w_key, w_value, gains], axis=1))
        kv_all = pack[:, : 2 * key_width]
        gain_cols = pack[:, 2 * key_width :].astype(F32)
        query_all = gather_rows(w_query)
        out_all = gather_rows(w_out)
        if in_slots:
            slots = slot_matrix(model_width)
            out_slots = slots if query_width == model_width else slot_matrix(query_width)
            to_slots = lambda value, matrix: dot(value, matrix).astype(BF16)
            from_slots = lambda value, matrix: dot_nt(value, matrix).astype(BF16)
            whole_from_slots = lambda value: lax.dot_general(
                value,
                slots.astype(F32),
                (((1,), (1,)), ((), ())),
                precision=lax.Precision.HIGHEST,
                preferred_element_type=F32,
            )
        else:
            slots = out_slots = None
            to_slots = from_slots = lambda value, matrix: value
            whole_from_slots = lambda value: value
        attn_gain_all = gain_cols[:, 0]
        ffn_gain_all = whole_from_slots(gain_cols[:, 1][None])[0]

        gate_up = jnp.concatenate(
            [
                w_gate.reshape(rows, dp_count, ffn_part),
                w_up.reshape(rows, dp_count, ffn_part),
            ],
            axis=2,
        )
        gate_up = lax.all_to_all(jnp.moveaxis(gate_up, 1, 0), "dp", 0, 0, tiled=True)
        down_all = lax.all_gather(w_down, "seq", axis=0, tiled=True)
        gate_up_all = lax.all_gather(gate_up, "seq", axis=1, tiled=True).reshape(
            model_width, 2 * ffn_part
        )
        cotangent_all = gather_dp(cotangent, dp_count)

        stream = tokens.astype(F32)
        scale_one = rms_scale(stream)
        stream_slots = to_slots(tokens, slots).astype(F32)
        normed_one = (stream_slots * scale_one * attn_gain_all).astype(BF16)
        positions = first_row + jnp.arange(local_len, dtype=jnp.int32)
        cosine_table, sine_table = rope_tables(positions, head_width)
        cosine_table = cosine_table[:, None, :]
        sine_table = sine_table[:, None, :]
        query_pre = dot(normed_one, query_all).reshape(local_len, query_heads, head_width)
        key_value = dot(normed_one, kv_all)
        key_pre = key_value[:, :key_width].reshape(local_len, key_heads, head_width)
        value_send = key_value[:, key_width:].astype(BF16)
        query_scale = rms_scale(query_pre)
        key_scale = rms_scale(key_pre)
        query_gain_f = query_gain.astype(F32)
        key_gain_f = key_gain.astype(F32)
        query_rot = rotate(
            query_pre * query_scale * query_gain_f, cosine_table, sine_table
        ).astype(BF16)
        key_rot = (
            rotate(key_pre * key_scale * key_gain_f, cosine_table, sine_table)
            .astype(BF16)
            .reshape(local_len, key_width)
        )

        both = [jnp.concatenate([key_rot, value_send], axis=1)]
        for _ in range(hops):
            both.append(shift_seq(both[-1], 2))
        for_even = jnp.concatenate(both[:-1], axis=0)
        for_odd = jnp.concatenate(both[1:], axis=0)
        across = swap_core(jnp.where(core == 0, for_even, for_odd))
        window = jnp.concatenate(both + [across], axis=0)
        block_steps = [-2 * i for i in range(hops + 1)] + [-1 - 2 * i for i in range(hops)]
        starts = [first_row + step * local_len for step in block_steps]
        key_pos = jnp.concatenate([start + jnp.arange(local_len, dtype=jnp.int32) for start in starts])
        key_ids = jnp.concatenate(
            [
                lax.dynamic_slice_in_dim(ids, jnp.maximum(start, 0), local_len, 0)
                for start in starts
            ]
        )
        query_ids = lax.dynamic_slice_in_dim(ids, first_row, local_len, 0)
        allowed = (
            (key_pos[None, :] <= positions[:, None])
            & (key_pos[None, :] >= 0)
            & (key_ids[None, :] == query_ids[:, None])
        )[None, None]
        window_len = window.shape[0]
        keys = window[:, :key_width].reshape(window_len, key_heads, head_width)
        values = window[:, key_width:].reshape(window_len, key_heads, head_width)
        queries = query_rot.reshape(local_len, key_heads, group_size, head_width)
        scores = (
            jnp.einsum("qgrd,kgd->grqk", queries, keys, preferred_element_type=F32)
            * softmax_scale
        )
        weights = jnp.where(allowed, jnp.exp(scores), 0.0)
        denominator = jnp.sum(weights, axis=-1)
        summed = jnp.einsum(
            "grqk,kgd->qgrd", weights.astype(BF16), values, preferred_element_type=F32
        )
        attended = (summed / jnp.moveaxis(denominator, 2, 0)[..., None]).astype(BF16)
        log_total = jnp.log(denominator)
        attended_flat = attended.reshape(local_len, query_width)
        attended_slots = to_slots(attended_flat, out_slots)
        middle = stream + dot(attended_slots, out_all)

        scale_two = rms_scale(middle)
        normed_two = (middle * scale_two * ffn_gain_all).astype(BF16)
        normed_all = gather_dp(normed_two, dp_count)
        both_pre = dot(normed_all, gate_up_all)
        gate_pre = both_pre[:, :ffn_part]
        up_pre = both_pre[:, ffn_part:]
        sigmoid_gate = jax.nn.sigmoid(gate_pre)
        silu_gate = gate_pre * sigmoid_gate
        hidden = (silu_gate * up_pre).astype(BF16)
        out_part = dot(hidden, down_all).astype(BF16)
        output = (middle + scatter_sum_dp(out_part, dp_count)).astype(BF16)
        grad_output = cotangent.astype(F32)
        grad_hidden = dot_nt(cotangent_all, down_all)
        grad_gate = (
            grad_hidden * up_pre * sigmoid_gate * (1.0 + gate_pre * (1.0 - sigmoid_gate))
        ).astype(BF16)
        grad_up = (grad_hidden * silu_gate).astype(BF16)
        grad_both = jnp.concatenate([grad_gate, grad_up], axis=1)
        grad_normed_two = scatter_sum_dp(dot_nt(grad_both, gate_up_all).astype(BF16), dp_count)
        grad_down_w = lax.psum_scatter(
            dot_tn(hidden, cotangent_all).astype(BF16), "seq", scatter_dimension=0, tiled=True
        )
        grad_gate_up = lax.psum_scatter(
            dot_tn(normed_all, grad_both)
            .astype(BF16)
            .reshape(dp_count, seq_shards * rows, 2 * ffn_part),
            "seq",
            scatter_dimension=1,
            tiled=True,
        )
        grad_gate_up = lax.all_to_all(grad_gate_up, "dp", 0, 0, tiled=True).astype(F32)
        grad_gate_up = jnp.moveaxis(grad_gate_up, 0, 1)
        grad_gate_w = grad_gate_up[..., :ffn_part].reshape(rows, ffn_width)
        grad_up_w = grad_gate_up[..., ffn_part:].reshape(rows, ffn_width)

        grad_mid_norm, grad_ffn_gain = norm_back(
            grad_normed_two, middle, scale_two, ffn_gain_all, (0,)
        )
        grad_middle = grad_output + grad_mid_norm

        grad_middle_bf = grad_middle.astype(BF16)
        grad_out_w = scatter_rows(dot_tn(attended_slots, grad_middle_bf).astype(BF16))
        grad_attended = from_slots(
            dot_nt(grad_middle_bf, out_all).astype(BF16), out_slots
        ).reshape(local_len, key_heads, group_size, head_width)
        delta_rows = jnp.moveaxis(
            jnp.sum(grad_attended.astype(F32) * attended.astype(F32), axis=-1), 0, 2
        )
        probabilities = jnp.where(allowed, jnp.exp(scores - log_total[..., None]), 0.0)
        grad_probs = jnp.einsum(
            "qgrd,kgd->grqk", grad_attended, values, preferred_element_type=F32
        )
        grad_scores = (probabilities * (grad_probs - delta_rows[..., None])).astype(BF16)
        value_term = jnp.einsum(
            "grqk,qgrd->kgd",
            probabilities.astype(BF16),
            grad_attended,
            preferred_element_type=F32,
        )
        key_term = (
            jnp.einsum("grqk,qgrd->kgd", grad_scores, queries, preferred_element_type=F32)
            * softmax_scale
        )
        grad_query = (
            jnp.einsum("grqk,kgd->qgrd", grad_scores, keys, preferred_element_type=F32)
            * softmax_scale
        )
        grad_window = jnp.concatenate(
            [
                key_term.reshape(window_len, key_width),
                value_term.reshape(window_len, key_width),
            ],
            axis=1,
        ).astype(BF16)
        split = (hops + 1) * local_len
        back = swap_core(grad_window[split:])
        zero = jnp.zeros((local_len, 2 * key_width), BF16)
        back = jnp.where(
            core == 0,
            jnp.concatenate([back, zero], axis=0),
            jnp.concatenate([zero, back], axis=0),
        )
        total = grad_window[:split].astype(F32) + back.astype(F32)
        running = total[hops * local_len :]
        for step in range(hops - 1, -1, -1):
            arrived = shift_seq(running.astype(BF16), -2)
            running = total[step * local_len : (step + 1) * local_len] + arrived.astype(F32)
        key_sum = running[:, :key_width]
        value_grad_bf = running[:, key_width:].astype(BF16)
        grad_qnorm = unrotate(
            grad_query.reshape(local_len, query_heads, head_width), cosine_table, sine_table
        )
        grad_qpre, grad_qgain = norm_back(
            grad_qnorm, query_pre, query_scale, query_gain_f, (0, 1)
        )
        grad_knorm = unrotate(
            key_sum.reshape(local_len, key_heads, head_width), cosine_table, sine_table
        )
        grad_kpre, grad_kgain = norm_back(grad_knorm, key_pre, key_scale, key_gain_f, (0, 1))
        query_bf = grad_qpre.reshape(local_len, query_width).astype(BF16)
        grad_query_w = scatter_rows(dot_tn(normed_one, query_bf).astype(BF16))
        kv_bf = jnp.concatenate(
            [grad_kpre.reshape(local_len, key_width).astype(BF16), value_grad_bf], axis=1
        )
        grad_kv_w = scatter_rows(dot_tn(normed_one, kv_bf).astype(BF16))
        grad_normed_one = dot_nt(query_bf, query_all) + dot_nt(kv_bf, kv_all)
        grad_stream, grad_attn_gain = norm_back(
            grad_normed_one, stream_slots, scale_one, attn_gain_all, (0,)
        )
        grad_stream = whole_from_slots(grad_stream)
        grad_attn_gain = whole_from_slots(grad_attn_gain[None])[0]
        grad_tokens = grad_middle + grad_stream

        devices = dp_count * seq_shards
        head_gains = jnp.concatenate([grad_qgain, grad_kgain])
        small = jnp.concatenate(
            [
                grad_attn_gain.reshape(devices, rows),
                grad_ffn_gain.reshape(devices, rows),
                jnp.broadcast_to(head_gains, (devices, 2 * head_width)),
            ],
            axis=1,
        )
        small = jnp.sum(lax.all_to_all(small, BOTH, 0, 0, tiled=True), axis=0)
        return (
            output[None],
            grad_tokens[None],
            grad_query_w,
            grad_kv_w[:, :key_width],
            grad_kv_w[:, key_width:],
            grad_out_w,
            small[:rows],
            small[2 * rows : 2 * rows + head_width],
            small[2 * rows + head_width :],
            grad_gate_w,
            grad_up_w,
            grad_down_w.astype(F32),
            small[rows : 2 * rows],
        )

    return body


def solution(mesh):
    in_specs = (
        P("dp", "seq", None),
        P("dp", None),
        P(BOTH, None),
        P(BOTH, None),
        P(BOTH, None),
        P(BOTH, None),
        P(BOTH),
        P(),
        P(),
        P(BOTH, None),
        P(BOTH, None),
        P(BOTH, None),
        P(BOTH),
        P("dp", "seq", None),
    )
    out_specs = (
        P("dp", "seq", None),
        P("dp", "seq", None),
        P(BOTH, None),
        P(BOTH, None),
        P(BOTH, None),
        P(BOTH, None),
        P(BOTH),
        P(),
        P(),
        P(BOTH, None),
        P(BOTH, None),
        P(BOTH, None),
        P(BOTH),
    )
    body = make_body(mesh.shape["dp"], mesh.shape["seq"])
    return jax.shard_map(body, mesh=mesh, in_specs=in_specs, out_specs=out_specs, check_vma=False)
```

```python
import jax
import jax.numpy as jnp
from jax import lax
from jax.sharding import PartitionSpec as P

EPSILON = 1e-05
ROPE_BASE = 1000000.0
F32 = jnp.float32
BF16 = jnp.bfloat16
BOTH = ("dp", "seq")


def rms_scale(values):
    return lax.rsqrt(jnp.mean(values * values, axis=-1, keepdims=True) + EPSILON)


def rope_tables(positions, head_width):
    half_width = head_width // 2
    frequency = ROPE_BASE ** (-(jnp.arange(half_width, dtype=F32) * 2.0 / head_width))
    angles = positions.astype(F32)[:, None] * frequency[None, :]
    return (jnp.cos(angles), jnp.sin(angles))


def rotate(values, cosine_table, sine_table):
    half_width = values.shape[-1] // 2
    front_half = values[..., :half_width]
    back_half = values[..., half_width:]
    return jnp.concatenate(
        [
            front_half * cosine_table - back_half * sine_table,
            back_half * cosine_table + front_half * sine_table,
        ],
        axis=-1,
    )


def unrotate(incoming, cosine_table, sine_table):
    return rotate(incoming, cosine_table, -sine_table)


def norm_back(incoming, values, scale_vec, gain_vector, sum_axes):
    upstream = incoming * gain_vector
    grad_values = scale_vec * (
        upstream
        - values * scale_vec * scale_vec * jnp.mean(upstream * values, axis=-1, keepdims=True)
    )
    grad_gain = jnp.sum(incoming * values * scale_vec, axis=sum_axes)
    return (grad_values, grad_gain)


def dot(left, right):
    return jnp.dot(left, right, preferred_element_type=F32)


def dot_tn(left, right):
    return lax.dot_general(left, right, (((0,), (0,)), ((), ())), preferred_element_type=F32)


def dot_nt(left, right):
    return lax.dot_general(left, right, (((1,), (1,)), ((), ())), preferred_element_type=F32)


def swap_dp(value, bits, count):
    return lax.ppermute(value, "dp", [(i, i ^ bits) for i in range(count)])


def after(value, *others):
    return lax.optimization_barrier((value, *others))[0]


def gather_parts(value, count):
    if count != 4:
        return [lax.all_gather(value, "dp", axis=0, tiled=True)]
    half = value.shape[0] // 2
    one = swap_dp(value, 1, count)
    two = swap_dp(value, 2, count)
    top = swap_dp(two[:half], 1, count)
    bottom = swap_dp(one[half:], 2, count)
    return [value, one, two, jnp.concatenate([top, bottom], axis=0)]


def gather_dp(value, count):
    return jnp.concatenate(gather_parts(value, count), axis=0)


def scatter_parts(parts, count, fill=()):
    if count != 4:
        total = lax.psum_scatter(parts[0], "dp", scatter_dimension=0, tiled=True).astype(F32)
        return (total, fill)
    own, one, two, far = parts
    half = own.shape[0] // 2
    top = swap_dp(far[:half], 1, count).astype(F32)
    bottom = swap_dp(far[half:], 2, count).astype(F32)
    two_sum = jnp.concatenate(
        [(two[:half].astype(F32) + top).astype(BF16), two[half:]], axis=0
    )
    one_sum = jnp.concatenate(
        [one[:half], (one[half:].astype(F32) + bottom).astype(BF16)], axis=0
    )
    from_one = swap_dp(one_sum, 1, count)
    from_two = swap_dp(two_sum, 2, count)
    if fill:
        from_one, from_two, *fill = lax.optimization_barrier((from_one, from_two, *fill))
    return (own.astype(F32) + from_one.astype(F32) + from_two.astype(F32), tuple(fill))


def scatter_sum_dp(value, count):
    if count != 4:
        return scatter_parts([value], count)[0]
    rows = value.shape[0] // 4
    return scatter_parts([value[i * rows : (i + 1) * rows] for i in range(4)], count)[0]


def xor_order(value, rank):
    split = value.reshape((2, 2) + value.shape[1:])
    split = jnp.where(rank & 2, split[::-1], split)
    split = jnp.where(rank & 1, split[:, ::-1], split)
    return split.reshape(value.shape)


def exchange_dp(value, count):
    if count != 4:
        return lax.all_to_all(value, "dp", 0, 0, tiled=True)
    rank = lax.axis_index("dp")
    value = xor_order(value, rank)
    value = jnp.stack([value[0]] + [swap_dp(value[j], j, count) for j in range(1, 4)])
    return xor_order(value, rank)


def make_body(dp_count, seq_shards):
    def shift_seq(value, step):
        pairs = [(i, i + step) for i in range(seq_shards) if 0 <= i + step < seq_shards]
        return lax.ppermute(value, "seq", pairs)

    def swap_core(value):
        return lax.ppermute(value, "seq", [(i, i ^ 1) for i in range(seq_shards)])

    def turn_seq(value, step):
        return lax.ppermute(
            value, "seq", [(i, (i + step) % seq_shards) for i in range(seq_shards)]
        )

    pairs = seq_shards // 2
    in_slots = dp_count == 4

    def slot_matrix(width):
        rows = width // (dp_count * seq_shards)
        slot_row = jnp.arange(width, dtype=jnp.int32)
        inner = slot_row % rows
        slot = slot_row // rows
        chip = (lax.axis_index("seq") // 2 + slot % pairs) % pairs
        peer = lax.axis_index("dp") ^ (slot // pairs % dp_count)
        core = (lax.axis_index("seq") % 2) ^ (slot // (pairs * dp_count))
        source = ((peer * seq_shards) + chip * 2 + core) * rows + inner
        return (slot_row[:, None] == source[None, :]).astype(BF16)

    def gather_line(value):
        if not in_slots:
            return value
        line = [value] + [turn_seq(value, -2 * k) for k in range(1, pairs)]
        return jnp.concatenate(line, axis=0)

    def gather_rest(line):
        if not in_slots:
            return lax.all_gather(line, BOTH, axis=0, tiled=True)
        plane = gather_dp(line, dp_count)
        return jnp.concatenate([plane, swap_core(plane)], axis=0)

    def scatter_rows(parts):
        if not in_slots:
            return lax.psum_scatter(parts, BOTH, scatter_dimension=0, tiled=True).astype(F32)
        half = parts.shape[0] // 2
        chip = (parts[:half].astype(F32) + swap_core(parts[half:]).astype(F32)).astype(BF16)
        line = scatter_sum_dp(chip, dp_count)
        rows = line.shape[0] // pairs
        total = line[:rows]
        for k in range(1, pairs):
            piece = line[k * rows : (k + 1) * rows].astype(BF16)
            total = total + turn_seq(piece, 2 * k).astype(F32)
        return total

    def body(
        tokens,
        segment_ids,
        w_query,
        w_key,
        w_value,
        w_out,
        attn_gain,
        query_gain,
        key_gain,
        w_gate,
        w_up,
        w_down,
        ffn_gain,
        cotangent,
    ):
        _, local_len, model_width = tokens.shape
        seq_len = segment_ids.shape[1]
        head_width = query_gain.shape[0]
        query_width = w_query.shape[1]
        key_width = w_key.shape[1]
        query_heads = query_width // head_width
        key_heads = key_width // head_width
        group_size = query_heads // key_heads
        softmax_scale = head_width ** (-0.5)
        rows = w_query.shape[0]
        ffn_width = w_gate.shape[1]
        ffn_part = ffn_width // dp_count
        seq_rank = lax.axis_index("seq")
        core = seq_rank % 2
        first_row = seq_rank * local_len
        tokens = tokens[0]
        cotangent = cotangent[0]
        ids = segment_ids[0]

        reach = -(-(seq_len // 2 - 1) // local_len)
        hops = -(-reach // 2)

        gains = jnp.stack([attn_gain, ffn_gain], axis=1)
        gains = jnp.pad(gains, ((0, 0), (0, 126)))
        pack_line = gather_line(jnp.concatenate([w_key, w_value, gains], axis=1))
        query_line = gather_line(after(w_query, pack_line))
        pack = gather_rest(pack_line)
        kv_all = pack[:, : 2 * key_width]
        gain_cols = pack[:, 2 * key_width :].astype(F32)
        query_all = gather_rest(after(query_line, pack))
        if in_slots:
            slots = slot_matrix(model_width)
            out_slots = slots if query_width == model_width else slot_matrix(query_width)
            to_slots = lambda value, matrix: dot(value, matrix).astype(BF16)
            from_slots = lambda value, matrix: dot_nt(value, matrix).astype(BF16)
            whole_from_slots = lambda value: lax.dot_general(
                value,
                slots.astype(F32),
                (((1,), (1,)), ((), ())),
                precision=lax.Precision.HIGHEST,
                preferred_element_type=F32,
            )
        else:
            slots = out_slots = None
            to_slots = from_slots = lambda value, matrix: value
            whole_from_slots = lambda value: value
        attn_gain_all = gain_cols[:, 0]
        ffn_gain_all = whole_from_slots(gain_cols[:, 1][None])[0]

        gate_up = jnp.concatenate(
            [
                w_gate.reshape(rows, dp_count, ffn_part),
                w_up.reshape(rows, dp_count, ffn_part),
            ],
            axis=2,
        )
        gate_up = exchange_dp(jnp.moveaxis(gate_up, 1, 0), dp_count)
        gate_up = after(gate_up, pack_line)
        down_all = lax.all_gather(after(w_down, gate_up), "seq", axis=0, tiled=True)
        gate_up_all = lax.all_gather(gate_up, "seq", axis=1, tiled=True).reshape(
            model_width, 2 * ffn_part
        )
        cotangent_parts = gather_parts(after(cotangent, query_all), dp_count)

        stream = tokens.astype(F32)
        scale_one = rms_scale(stream)
        stream_slots = to_slots(tokens, slots).astype(F32)
        normed_one = (stream_slots * scale_one * attn_gain_all).astype(BF16)
        positions = first_row + jnp.arange(local_len, dtype=jnp.int32)
        cosine_table, sine_table = rope_tables(positions, head_width)
        cosine_table = cosine_table[:, None, :]
        sine_table = sine_table[:, None, :]
        query_pre = dot(normed_one, query_all).reshape(local_len, query_heads, head_width)
        key_value = dot(normed_one, kv_all)
        key_pre = key_value[:, :key_width].reshape(local_len, key_heads, head_width)
        value_send = key_value[:, key_width:].astype(BF16)
        query_scale = rms_scale(query_pre)
        key_scale = rms_scale(key_pre)
        query_gain_f = query_gain.astype(F32)
        key_gain_f = key_gain.astype(F32)
        query_rot = rotate(
            query_pre * query_scale * query_gain_f, cosine_table, sine_table
        ).astype(BF16)
        key_rot = (
            rotate(key_pre * key_scale * key_gain_f, cosine_table, sine_table)
            .astype(BF16)
            .reshape(local_len, key_width)
        )

        both = [jnp.concatenate([key_rot, value_send], axis=1)]
        for _ in range(hops):
            both.append(shift_seq(both[-1], 2))
        out_all = gather_rest(gather_line(after(w_out, both[-1])))
        for_even = jnp.concatenate(both[:-1], axis=0)
        for_odd = jnp.concatenate(both[1:], axis=0)
        across = swap_core(jnp.where(core == 0, for_even, for_odd))
        window = jnp.concatenate(both + [across], axis=0)
        block_steps = [-2 * i for i in range(hops + 1)] + [-1 - 2 * i for i in range(hops)]
        starts = [first_row + step * local_len for step in block_steps]
        key_pos = jnp.concatenate([start + jnp.arange(local_len, dtype=jnp.int32) for start in starts])
        key_ids = jnp.concatenate(
            [
                lax.dynamic_slice_in_dim(ids, jnp.maximum(start, 0), local_len, 0)
                for start in starts
            ]
        )
        query_ids = lax.dynamic_slice_in_dim(ids, first_row, local_len, 0)
        allowed = (
            (key_pos[None, :] <= positions[:, None])
            & (key_pos[None, :] >= 0)
            & (key_ids[None, :] == query_ids[:, None])
        )[None, None]
        window_len = window.shape[0]
        keys = window[:, :key_width].reshape(window_len, key_heads, head_width)
        values = window[:, key_width:].reshape(window_len, key_heads, head_width)
        queries = query_rot.reshape(local_len, key_heads, group_size, head_width)
        scores = (
            jnp.einsum("qgrd,kgd->grqk", queries, keys, preferred_element_type=F32)
            * softmax_scale
        )
        weights = jnp.where(allowed, jnp.exp(scores), 0.0)
        denominator = jnp.sum(weights, axis=-1)
        summed = jnp.einsum(
            "grqk,kgd->qgrd", weights.astype(BF16), values, preferred_element_type=F32
        )
        attended = (summed / jnp.moveaxis(denominator, 2, 0)[..., None]).astype(BF16)
        log_total = jnp.log(denominator)
        attended_flat = attended.reshape(local_len, query_width)
        attended_slots = to_slots(attended_flat, out_slots)
        middle = stream + dot(attended_slots, out_all)

        scale_two = rms_scale(middle)
        normed_two = (middle * scale_two * ffn_gain_all).astype(BF16)
        normed_parts = gather_parts(normed_two, dp_count)

        def chunked(parts):
            if len(parts) == 1:
                return list(parts)
            own, one, two, far = parts
            return [own, jnp.concatenate([one, two], axis=0), far]

        def whole(chunks):
            return chunks[0] if len(chunks) == 1 else jnp.concatenate(chunks, axis=0)

        def parts_of(chunks):
            if len(chunks) == 1:
                return list(chunks)
            own, middle_two, far = chunks
            return [own, middle_two[:local_len], middle_two[local_len:], far]

        normed_chunks = chunked(normed_parts)
        cotangent_chunks = chunked(cotangent_parts)
        saved = []
        hidden_chunks = []
        for chunk in normed_chunks:
            both_pre = dot(chunk, gate_up_all)
            gate_pre = both_pre[:, :ffn_part]
            up_pre = both_pre[:, ffn_part:]
            sigmoid_gate = jax.nn.sigmoid(gate_pre)
            silu_gate = gate_pre * sigmoid_gate
            hidden_chunks.append((silu_gate * up_pre).astype(BF16))
            saved.append((gate_pre, up_pre, sigmoid_gate, silu_gate))
        grad_output = cotangent.astype(F32)
        grad_chunks = [None] * len(saved)
        back_chunks = [None] * len(saved)
        previous = None
        for i in reversed(range(len(saved))):
            gate_pre, up_pre, sigmoid_gate, silu_gate = saved[i]
            incoming = cotangent_chunks[i]
            if previous is not None:
                incoming = after(incoming, previous)
            grad_hidden = dot_nt(incoming, down_all)
            grad_gate = (
                grad_hidden * up_pre * sigmoid_gate * (1.0 + gate_pre * (1.0 - sigmoid_gate))
            ).astype(BF16)
            grad_up = (grad_hidden * silu_gate).astype(BF16)
            grad_chunks[i] = jnp.concatenate([grad_gate, grad_up], axis=1)
            back_chunks[i] = dot_nt(grad_chunks[i], gate_up_all).astype(BF16)
            previous = back_chunks[i]
        hidden = whole(hidden_chunks)
        grad_both = whole(grad_chunks)
        normed_all = whole(normed_chunks)
        cotangent_all = whole(cotangent_chunks)
        gate_up_part = dot_tn(normed_all, grad_both).astype(BF16)
        down_part = dot_tn(hidden, cotangent_all).astype(BF16)
        grad_normed_two, (gate_up_part, down_part) = scatter_parts(
            parts_of(back_chunks), dp_count, (gate_up_part, down_part)
        )
        grad_gate_up = lax.psum_scatter(
            gate_up_part.reshape(dp_count, seq_shards * rows, 2 * ffn_part),
            "seq",
            scatter_dimension=1,
            tiled=True,
        )
        grad_down_w = lax.psum_scatter(
            after(down_part, gate_up_part), "seq", scatter_dimension=0, tiled=True
        )
        out_chunks = [dot(chunk, down_all).astype(BF16) for chunk in hidden_chunks]
        output = (middle + scatter_parts(parts_of(out_chunks), dp_count)[0]).astype(BF16)
        grad_gate_up = exchange_dp(grad_gate_up, dp_count)
        grad_gate_up = jnp.moveaxis(grad_gate_up.astype(F32), 0, 1)
        grad_gate_w = grad_gate_up[..., :ffn_part].reshape(rows, ffn_width)
        grad_up_w = grad_gate_up[..., ffn_part:].reshape(rows, ffn_width)

        grad_mid_norm, grad_ffn_gain = norm_back(
            grad_normed_two, middle, scale_two, ffn_gain_all, (0,)
        )
        grad_middle = grad_output + grad_mid_norm

        grad_middle_bf = grad_middle.astype(BF16)
        grad_out_w = scatter_rows(dot_tn(attended_slots, grad_middle_bf).astype(BF16))
        grad_attended = from_slots(
            dot_nt(grad_middle_bf, out_all).astype(BF16), out_slots
        ).reshape(local_len, key_heads, group_size, head_width)
        delta_rows = jnp.moveaxis(
            jnp.sum(grad_attended.astype(F32) * attended.astype(F32), axis=-1), 0, 2
        )
        probabilities = jnp.where(allowed, jnp.exp(scores - log_total[..., None]), 0.0)
        grad_probs = jnp.einsum(
            "qgrd,kgd->grqk", grad_attended, values, preferred_element_type=F32
        )
        grad_scores = (probabilities * (grad_probs - delta_rows[..., None])).astype(BF16)
        value_term = jnp.einsum(
            "grqk,qgrd->kgd",
            probabilities.astype(BF16),
            grad_attended,
            preferred_element_type=F32,
        )
        key_term = (
            jnp.einsum("grqk,qgrd->kgd", grad_scores, queries, preferred_element_type=F32)
            * softmax_scale
        )
        grad_query = (
            jnp.einsum("grqk,kgd->qgrd", grad_scores, keys, preferred_element_type=F32)
            * softmax_scale
        )
        grad_window = jnp.concatenate(
            [
                key_term.reshape(window_len, key_width),
                value_term.reshape(window_len, key_width),
            ],
            axis=1,
        ).astype(BF16)
        grad_window, grad_out_w = lax.optimization_barrier((grad_window, grad_out_w))
        split = (hops + 1) * local_len
        back = swap_core(grad_window[split:])
        zero = jnp.zeros((local_len, 2 * key_width), BF16)
        back = jnp.where(
            core == 0,
            jnp.concatenate([back, zero], axis=0),
            jnp.concatenate([zero, back], axis=0),
        )
        total = grad_window[:split].astype(F32) + back.astype(F32)
        running = total[hops * local_len :]
        for step in range(hops - 1, -1, -1):
            arrived = shift_seq(running.astype(BF16), -2)
            running = total[step * local_len : (step + 1) * local_len] + arrived.astype(F32)
        key_sum = running[:, :key_width]
        value_grad_bf = running[:, key_width:].astype(BF16)
        grad_qnorm = unrotate(
            grad_query.reshape(local_len, query_heads, head_width), cosine_table, sine_table
        )
        grad_qpre, grad_qgain = norm_back(
            grad_qnorm, query_pre, query_scale, query_gain_f, (0, 1)
        )
        grad_knorm = unrotate(
            key_sum.reshape(local_len, key_heads, head_width), cosine_table, sine_table
        )
        grad_kpre, grad_kgain = norm_back(grad_knorm, key_pre, key_scale, key_gain_f, (0, 1))
        query_bf = grad_qpre.reshape(local_len, query_width).astype(BF16)
        grad_query_w = scatter_rows(dot_tn(normed_one, query_bf).astype(BF16))
        kv_bf = jnp.concatenate(
            [grad_kpre.reshape(local_len, key_width).astype(BF16), value_grad_bf], axis=1
        )
        grad_kv_w = scatter_rows(dot_tn(normed_one, kv_bf).astype(BF16))
        grad_normed_one = dot_nt(query_bf, query_all) + dot_nt(kv_bf, kv_all)
        grad_stream, grad_attn_gain = norm_back(
            grad_normed_one, stream_slots, scale_one, attn_gain_all, (0,)
        )
        grad_stream = whole_from_slots(grad_stream)
        grad_attn_gain = whole_from_slots(grad_attn_gain[None])[0]
        grad_tokens = grad_middle + grad_stream

        devices = dp_count * seq_shards
        head_gains = jnp.concatenate([grad_qgain, grad_kgain])
        small = jnp.concatenate(
            [
                grad_attn_gain.reshape(devices, rows),
                grad_ffn_gain.reshape(devices, rows),
                jnp.broadcast_to(head_gains, (devices, 2 * head_width)),
            ],
            axis=1,
        )
        small = jnp.sum(lax.all_to_all(small, BOTH, 0, 0, tiled=True), axis=0)
        return (
            output[None],
            grad_tokens[None],
            grad_query_w,
            grad_kv_w[:, :key_width],
            grad_kv_w[:, key_width:],
            grad_out_w,
            small[:rows],
            small[2 * rows : 2 * rows + head_width],
            small[2 * rows + head_width :],
            grad_gate_w,
            grad_up_w,
            grad_down_w.astype(F32),
            small[rows : 2 * rows],
        )

    return body


def solution(mesh):
    in_specs = (
        P("dp", "seq", None),
        P("dp", None),
        P(BOTH, None),
        P(BOTH, None),
        P(BOTH, None),
        P(BOTH, None),
        P(BOTH),
        P(),
        P(),
        P(BOTH, None),
        P(BOTH, None),
        P(BOTH, None),
        P(BOTH),
        P("dp", "seq", None),
    )
    out_specs = (
        P("dp", "seq", None),
        P("dp", "seq", None),
        P(BOTH, None),
        P(BOTH, None),
        P(BOTH, None),
        P(BOTH, None),
        P(BOTH),
        P(),
        P(),
        P(BOTH, None),
        P(BOTH, None),
        P(BOTH, None),
        P(BOTH),
    )
    body = make_body(mesh.shape["dp"], mesh.shape["seq"])
    return jax.shard_map(body, mesh=mesh, in_specs=in_specs, out_specs=out_specs, check_vma=False)
```

```python
import jax
import jax.numpy as jnp
from jax import lax
from jax.sharding import PartitionSpec as P

EPSILON = 1e-05
ROPE_BASE = 1000000.0
F32 = jnp.float32
BF16 = jnp.bfloat16
BOTH = ("dp", "seq")


def rms_scale(values):
    return lax.rsqrt(jnp.mean(values * values, axis=-1, keepdims=True) + EPSILON)


def rope_tables(positions, head_width):
    half_width = head_width // 2
    frequency = ROPE_BASE ** (-(jnp.arange(half_width, dtype=F32) * 2.0 / head_width))
    angles = positions.astype(F32)[:, None] * frequency[None, :]
    return (jnp.cos(angles), jnp.sin(angles))


def rotate(values, cosine_table, sine_table):
    half_width = values.shape[-1] // 2
    front_half = values[..., :half_width]
    back_half = values[..., half_width:]
    return jnp.concatenate(
        [
            front_half * cosine_table - back_half * sine_table,
            back_half * cosine_table + front_half * sine_table,
        ],
        axis=-1,
    )


def unrotate(incoming, cosine_table, sine_table):
    return rotate(incoming, cosine_table, -sine_table)


def norm_back(incoming, values, scale_vec, gain_vector, sum_axes):
    upstream = incoming * gain_vector
    grad_values = scale_vec * (
        upstream
        - values * scale_vec * scale_vec * jnp.mean(upstream * values, axis=-1, keepdims=True)
    )
    grad_gain = jnp.sum(incoming * values * scale_vec, axis=sum_axes)
    return (grad_values, grad_gain)


def dot(left, right):
    return jnp.dot(left, right, preferred_element_type=F32)


def dot_tn(left, right):
    return lax.dot_general(left, right, (((0,), (0,)), ((), ())), preferred_element_type=F32)


def dot_nt(left, right):
    return lax.dot_general(left, right, (((1,), (1,)), ((), ())), preferred_element_type=F32)


def swap_dp(value, bits, count):
    return lax.ppermute(value, "dp", [(i, i ^ bits) for i in range(count)])


def after(value, *others):
    return lax.optimization_barrier((value, *others))[0]


def gather_parts(value, count):
    if count != 4:
        return [lax.all_gather(value, "dp", axis=0, tiled=True)]
    half = value.shape[0] // 2
    one = swap_dp(value, 1, count)
    two = swap_dp(value, 2, count)
    top = swap_dp(two[:half], 1, count)
    bottom = swap_dp(one[half:], 2, count)
    return [value, one, two, jnp.concatenate([top, bottom], axis=0)]


def gather_dp(value, count):
    return jnp.concatenate(gather_parts(value, count), axis=0)


def scatter_steps(parts, count):
    if count != 4:
        return lax.psum_scatter(parts[0], "dp", scatter_dimension=0, tiled=True).astype(F32)
    own, one, two, far = parts
    half = own.shape[0] // 2
    top, bottom = yield (swap_dp(far[:half], 1, count), swap_dp(far[half:], 2, count))
    two_sum = jnp.concatenate(
        [(two[:half].astype(F32) + top.astype(F32)).astype(BF16), two[half:]], axis=0
    )
    one_sum = jnp.concatenate(
        [one[:half], (one[half:].astype(F32) + bottom.astype(F32)).astype(BF16)], axis=0
    )
    from_one, from_two = yield (swap_dp(one_sum, 1, count), swap_dp(two_sum, 2, count))
    return own.astype(F32) + from_one.astype(F32) + from_two.astype(F32)


def run_steps(steps, ties=()):
    tied = []
    ties = list(ties)
    try:
        arrived = next(steps)
        while True:
            if ties:
                held = ties.pop(0)(tied)
                joined = lax.optimization_barrier((*arrived, *held))
                arrived = joined[: len(arrived)]
                tied.append(joined[len(arrived) :])
            arrived = steps.send(tuple(arrived))
    except StopIteration as stop:
        result = stop.value
    for tie in ties:
        tied.append(tuple(tie(tied)))
    return result, tied


def split_rows(value, count):
    if count != 4:
        return [value]
    rows = value.shape[0] // 4
    return [value[i * rows : (i + 1) * rows] for i in range(4)]


def scatter_sum_dp(value, count):
    return run_steps(scatter_steps(split_rows(value, count), count))[0]


def xor_order(value, rank):
    split = value.reshape((2, 2) + value.shape[1:])
    split = jnp.where(rank & 2, split[::-1], split)
    split = jnp.where(rank & 1, split[:, ::-1], split)
    return split.reshape(value.shape)


def exchange_dp(value, count):
    if count != 4:
        return lax.all_to_all(value, "dp", 0, 0, tiled=True)
    rank = lax.axis_index("dp")
    value = xor_order(value, rank)
    value = jnp.stack([value[0]] + [swap_dp(value[j], j, count) for j in range(1, 4)])
    return xor_order(value, rank)


def make_body(dp_count, seq_shards):
    def shift_seq(value, step):
        pairs = [(i, i + step) for i in range(seq_shards) if 0 <= i + step < seq_shards]
        return lax.ppermute(value, "seq", pairs)

    def swap_core(value):
        return lax.ppermute(value, "seq", [(i, i ^ 1) for i in range(seq_shards)])

    def turn_seq(value, step):
        return lax.ppermute(
            value, "seq", [(i, (i + step) % seq_shards) for i in range(seq_shards)]
        )

    pairs = seq_shards // 2
    in_slots = dp_count == 4

    def slot_matrix(width):
        rows = width // (dp_count * seq_shards)
        slot_row = jnp.arange(width, dtype=jnp.int32)
        inner = slot_row % rows
        slot = slot_row // rows
        chip = (lax.axis_index("seq") // 2 + slot % pairs) % pairs
        peer = lax.axis_index("dp") ^ (slot // pairs % dp_count)
        core = (lax.axis_index("seq") % 2) ^ (slot // (pairs * dp_count))
        source = ((peer * seq_shards) + chip * 2 + core) * rows + inner
        return (slot_row[:, None] == source[None, :]).astype(BF16)

    def gather_line(value):
        if not in_slots:
            return value
        line = [value] + [turn_seq(value, -2 * k) for k in range(1, pairs)]
        return jnp.concatenate(line, axis=0)

    def gather_rest(line):
        if not in_slots:
            return lax.all_gather(line, BOTH, axis=0, tiled=True)
        plane = gather_dp(line, dp_count)
        return jnp.concatenate([plane, swap_core(plane)], axis=0)

    def scatter_row_steps(parts):
        if not in_slots:
            return lax.psum_scatter(parts, BOTH, scatter_dimension=0, tiled=True).astype(F32)
        half = parts.shape[0] // 2
        (other,) = yield (swap_core(parts[half:]),)
        chip = (parts[:half].astype(F32) + other.astype(F32)).astype(BF16)
        line = yield from scatter_steps(split_rows(chip, dp_count), dp_count)
        rows = line.shape[0] // pairs
        total = line[:rows]
        for k in range(1, pairs):
            piece = line[k * rows : (k + 1) * rows].astype(BF16)
            total = total + turn_seq(piece, 2 * k).astype(F32)
        return total

    def scatter_rows(parts):
        return run_steps(scatter_row_steps(parts))[0]

    def body(
        tokens,
        segment_ids,
        w_query,
        w_key,
        w_value,
        w_out,
        attn_gain,
        query_gain,
        key_gain,
        w_gate,
        w_up,
        w_down,
        ffn_gain,
        cotangent,
    ):
        _, local_len, model_width = tokens.shape
        seq_len = segment_ids.shape[1]
        head_width = query_gain.shape[0]
        query_width = w_query.shape[1]
        key_width = w_key.shape[1]
        query_heads = query_width // head_width
        key_heads = key_width // head_width
        group_size = query_heads // key_heads
        softmax_scale = head_width ** (-0.5)
        rows = w_query.shape[0]
        ffn_width = w_gate.shape[1]
        ffn_part = ffn_width // dp_count
        seq_rank = lax.axis_index("seq")
        core = seq_rank % 2
        first_row = seq_rank * local_len
        tokens = tokens[0]
        cotangent = cotangent[0]
        ids = segment_ids[0]

        reach = -(-(seq_len // 2 - 1) // local_len)
        hops = -(-reach // 2)

        gains = jnp.stack([attn_gain, ffn_gain], axis=1)
        gains = jnp.pad(gains, ((0, 0), (0, 126)))
        pack_line = gather_line(jnp.concatenate([w_key, w_value, gains], axis=1))
        query_line = gather_line(after(w_query, pack_line))
        pack = gather_rest(pack_line)
        kv_all = pack[:, : 2 * key_width]
        gain_cols = pack[:, 2 * key_width :].astype(F32)
        query_all = gather_rest(after(query_line, pack))
        out_all = gather_rest(gather_line(after(w_out, query_line)))
        if in_slots:
            slots = slot_matrix(model_width)
            out_slots = slots if query_width == model_width else slot_matrix(query_width)
            to_slots = lambda value, matrix: dot(value, matrix).astype(BF16)
            from_slots = lambda value, matrix: dot_nt(value, matrix).astype(BF16)
            whole_from_slots = lambda value: lax.dot_general(
                value,
                slots.astype(F32),
                (((1,), (1,)), ((), ())),
                precision=lax.Precision.HIGHEST,
                preferred_element_type=F32,
            )
        else:
            slots = out_slots = None
            to_slots = from_slots = lambda value, matrix: value
            whole_from_slots = lambda value: value
        attn_gain_all = gain_cols[:, 0]
        ffn_gain_all = whole_from_slots(gain_cols[:, 1][None])[0]

        gate_up = jnp.concatenate(
            [
                w_gate.reshape(rows, dp_count, ffn_part),
                w_up.reshape(rows, dp_count, ffn_part),
            ],
            axis=2,
        )
        gate_up = exchange_dp(jnp.moveaxis(gate_up, 1, 0), dp_count)
        gate_up = after(gate_up, pack_line)
        down_all = lax.all_gather(after(w_down, gate_up), "seq", axis=0, tiled=True)
        gate_up_all = lax.all_gather(gate_up, "seq", axis=1, tiled=True).reshape(
            model_width, 2 * ffn_part
        )
        cotangent_parts = gather_parts(after(cotangent, pack), dp_count)

        stream = tokens.astype(F32)
        scale_one = rms_scale(stream)
        stream_slots = to_slots(tokens, slots).astype(F32)
        normed_one = (stream_slots * scale_one * attn_gain_all).astype(BF16)
        positions = first_row + jnp.arange(local_len, dtype=jnp.int32)
        cosine_table, sine_table = rope_tables(positions, head_width)
        cosine_table = cosine_table[:, None, :]
        sine_table = sine_table[:, None, :]
        query_pre = dot(normed_one, query_all).reshape(local_len, query_heads, head_width)
        key_value = dot(normed_one, kv_all)
        key_pre = key_value[:, :key_width].reshape(local_len, key_heads, head_width)
        value_send = key_value[:, key_width:].astype(BF16)
        query_scale = rms_scale(query_pre)
        key_scale = rms_scale(key_pre)
        query_gain_f = query_gain.astype(F32)
        key_gain_f = key_gain.astype(F32)
        query_rot = rotate(
            query_pre * query_scale * query_gain_f, cosine_table, sine_table
        ).astype(BF16)
        key_rot = (
            rotate(key_pre * key_scale * key_gain_f, cosine_table, sine_table)
            .astype(BF16)
            .reshape(local_len, key_width)
        )

        both = [jnp.concatenate([key_rot, value_send], axis=1)]
        for _ in range(hops):
            both.append(shift_seq(both[-1], 2))
        for_even = jnp.concatenate(both[:-1], axis=0)
        for_odd = jnp.concatenate(both[1:], axis=0)
        across = swap_core(jnp.where(core == 0, for_even, for_odd))
        window = jnp.concatenate(both + [across], axis=0)
        block_steps = [-2 * i for i in range(hops + 1)] + [-1 - 2 * i for i in range(hops)]
        starts = [first_row + step * local_len for step in block_steps]
        key_pos = jnp.concatenate([start + jnp.arange(local_len, dtype=jnp.int32) for start in starts])
        key_ids = jnp.concatenate(
            [
                lax.dynamic_slice_in_dim(ids, jnp.maximum(start, 0), local_len, 0)
                for start in starts
            ]
        )
        query_ids = lax.dynamic_slice_in_dim(ids, first_row, local_len, 0)
        allowed = (
            (key_pos[None, :] <= positions[:, None])
            & (key_pos[None, :] >= 0)
            & (key_ids[None, :] == query_ids[:, None])
        )[None, None]
        window_len = window.shape[0]
        keys = window[:, :key_width].reshape(window_len, key_heads, head_width)
        values = window[:, key_width:].reshape(window_len, key_heads, head_width)
        queries = query_rot.reshape(local_len, key_heads, group_size, head_width)
        scores = (
            jnp.einsum("qgrd,kgd->grqk", queries, keys, preferred_element_type=F32)
            * softmax_scale
        )
        weights = jnp.where(allowed, jnp.exp(scores), 0.0)
        denominator = jnp.sum(weights, axis=-1)
        summed = jnp.einsum(
            "grqk,kgd->qgrd", weights.astype(BF16), values, preferred_element_type=F32
        )
        attended = (summed / jnp.moveaxis(denominator, 2, 0)[..., None]).astype(BF16)
        log_total = jnp.log(denominator)
        attended_flat = attended.reshape(local_len, query_width)
        attended_slots = to_slots(attended_flat, out_slots)
        middle = stream + dot(attended_slots, out_all)

        scale_two = rms_scale(middle)
        normed_two = (middle * scale_two * ffn_gain_all).astype(BF16)
        def chunked(parts):
            if len(parts) == 1:
                return list(parts)
            own, one, two, far = parts
            return [own, jnp.concatenate([one, two], axis=0), far]

        def whole(chunks):
            return chunks[0] if len(chunks) == 1 else jnp.concatenate(chunks, axis=0)

        def parts_of(chunks):
            if len(chunks) == 1:
                return list(chunks)
            own, middle_two, far = chunks
            return [own, middle_two[:local_len], middle_two[local_len:], far]

        def forward(chunk):
            both_pre = dot(chunk, gate_up_all)
            gate_pre = both_pre[:, :ffn_part]
            up_pre = both_pre[:, ffn_part:]
            sigmoid_gate = jax.nn.sigmoid(gate_pre)
            silu_gate = gate_pre * sigmoid_gate
            hidden = (silu_gate * up_pre).astype(BF16)
            return hidden, (gate_pre, up_pre, sigmoid_gate, silu_gate)

        cotangent_chunks = chunked(cotangent_parts)
        if dp_count == 4:
            half = local_len // 2
            one = swap_dp(normed_two, 1, dp_count)
            two = swap_dp(normed_two, 2, dp_count)
            first = forward(normed_two)
            one, two, own_hidden = lax.optimization_barrier((one, two, first[0]))
            top = swap_dp(two[:half], 1, dp_count)
            bottom = swap_dp(one[half:], 2, dp_count)
            near = jnp.concatenate([one, two], axis=0)
            second = forward(near)
            top, bottom, near_hidden = lax.optimization_barrier((top, bottom, second[0]))
            far = jnp.concatenate([top, bottom], axis=0)
            third = forward(far)
            normed_chunks = [normed_two, near, far]
            hidden_chunks = [own_hidden, near_hidden, third[0]]
            saved = [first[1], second[1], third[1]]
        else:
            normed_chunks = [lax.all_gather(normed_two, "dp", axis=0, tiled=True)]
            hidden_all, kept = forward(normed_chunks[0])
            hidden_chunks = [hidden_all]
            saved = [kept]
        grad_output = cotangent.astype(F32)
        grad_chunks = [None] * len(saved)
        back_chunks = [None] * len(saved)
        previous = None
        for i in reversed(range(len(saved))):
            gate_pre, up_pre, sigmoid_gate, silu_gate = saved[i]
            incoming = cotangent_chunks[i]
            if previous is not None:
                incoming = after(incoming, previous)
            grad_hidden = dot_nt(incoming, down_all)
            grad_gate = (
                grad_hidden * up_pre * sigmoid_gate * (1.0 + gate_pre * (1.0 - sigmoid_gate))
            ).astype(BF16)
            grad_up = (grad_hidden * silu_gate).astype(BF16)
            grad_chunks[i] = jnp.concatenate([grad_gate, grad_up], axis=1)
            back_chunks[i] = dot_nt(grad_chunks[i], gate_up_all).astype(BF16)
            previous = back_chunks[i]
        hidden = whole(hidden_chunks)
        grad_both = whole(grad_chunks)
        normed_all = whole(normed_chunks)
        cotangent_all = whole(cotangent_chunks)
        grad_normed_two, tied = run_steps(
            scatter_steps(parts_of(back_chunks), dp_count),
            (
                lambda tied: (hidden, grad_both, normed_all, cotangent_all),
                lambda tied: (
                    dot_tn(tied[0][2], tied[0][1]).astype(BF16),
                    dot_tn(tied[0][0], tied[0][3]).astype(BF16),
                ),
            ),
        )
        gate_up_part, down_part = tied[1]
        grad_gate_up = lax.psum_scatter(
            gate_up_part.reshape(dp_count, seq_shards * rows, 2 * ffn_part),
            "seq",
            scatter_dimension=1,
            tiled=True,
        )
        grad_down_w = lax.psum_scatter(
            after(down_part, gate_up_part), "seq", scatter_dimension=0, tiled=True
        )
        out_chunks = [dot(chunk, down_all).astype(BF16) for chunk in hidden_chunks]
        output = run_steps(scatter_steps(parts_of(out_chunks), dp_count))[0]
        output = (middle + output).astype(BF16)
        grad_mid_norm, grad_ffn_gain = norm_back(
            grad_normed_two, middle, scale_two, ffn_gain_all, (0,)
        )
        grad_middle = grad_output + grad_mid_norm

        grad_middle_bf = grad_middle.astype(BF16)
        out_steps = scatter_row_steps(dot_tn(attended_slots, grad_middle_bf).astype(BF16))
        grad_attended = from_slots(
            dot_nt(grad_middle_bf, out_all).astype(BF16), out_slots
        ).reshape(local_len, key_heads, group_size, head_width)
        delta_rows = jnp.moveaxis(
            jnp.sum(grad_attended.astype(F32) * attended.astype(F32), axis=-1), 0, 2
        )
        probabilities = jnp.where(allowed, jnp.exp(scores - log_total[..., None]), 0.0)
        grad_probs = jnp.einsum(
            "qgrd,kgd->grqk", grad_attended, values, preferred_element_type=F32
        )
        grad_scores = (probabilities * (grad_probs - delta_rows[..., None])).astype(BF16)
        def query_and_key_term(grad_scores):
            key_term = (
                jnp.einsum("grqk,qgrd->kgd", grad_scores, queries, preferred_element_type=F32)
                * softmax_scale
            )
            grad_query = (
                jnp.einsum("grqk,kgd->qgrd", grad_scores, keys, preferred_element_type=F32)
                * softmax_scale
            )
            return (grad_query, key_term)

        value_term = jnp.einsum(
            "grqk,qgrd->kgd",
            probabilities.astype(BF16),
            grad_attended,
            preferred_element_type=F32,
        )
        grad_out_w, tied = run_steps(
            out_steps,
            (lambda tied: (grad_scores,), lambda tied: query_and_key_term(*tied[0])),
        )
        grad_query, key_term = tied[1]
        grad_window = jnp.concatenate(
            [
                key_term.reshape(window_len, key_width),
                value_term.reshape(window_len, key_width),
            ],
            axis=1,
        ).astype(BF16)
        split = (hops + 1) * local_len
        back = swap_core(grad_window[split:])
        arrived_back = back
        zero = jnp.zeros((local_len, 2 * key_width), BF16)
        back = jnp.where(
            core == 0,
            jnp.concatenate([back, zero], axis=0),
            jnp.concatenate([zero, back], axis=0),
        )
        total = grad_window[:split].astype(F32) + back.astype(F32)
        running = total[hops * local_len :]
        for step in range(hops - 1, -1, -1):
            arrived = shift_seq(running.astype(BF16), -2)
            if step == 0:
                arrived, grad_gate_up = lax.optimization_barrier((arrived, grad_gate_up))
            running = total[step * local_len : (step + 1) * local_len] + arrived.astype(F32)
        key_sum = running[:, :key_width]
        value_grad_bf = running[:, key_width:].astype(BF16)
        grad_qnorm = unrotate(
            grad_query.reshape(local_len, query_heads, head_width), cosine_table, sine_table
        )
        grad_qpre, grad_qgain = norm_back(
            grad_qnorm, query_pre, query_scale, query_gain_f, (0, 1)
        )
        grad_knorm = unrotate(
            key_sum.reshape(local_len, key_heads, head_width), cosine_table, sine_table
        )
        grad_kpre, grad_kgain = norm_back(grad_knorm, key_pre, key_scale, key_gain_f, (0, 1))
        query_bf = grad_qpre.reshape(local_len, query_width).astype(BF16)
        grad_query_w = scatter_rows(
            after(dot_tn(normed_one, query_bf).astype(BF16), arrived_back)
        )
        kv_bf = jnp.concatenate(
            [grad_kpre.reshape(local_len, key_width).astype(BF16), value_grad_bf], axis=1
        )
        kv_part = dot_tn(normed_one, kv_bf).astype(BF16)
        kv_after = after(kv_bf, kv_part)

        def last_norm_back(tied):
            (grad_normed_one,) = tied[0]
            grad_stream, grad_attn_gain = norm_back(
                grad_normed_one, stream_slots, scale_one, attn_gain_all, (0,)
            )
            return (
                whole_from_slots(grad_stream),
                whole_from_slots(grad_attn_gain[None])[0],
            )

        grad_kv_w, tied = run_steps(
            scatter_row_steps(kv_part),
            (
                lambda tied: (dot_nt(query_bf, query_all) + dot_nt(kv_after, kv_all),),
                last_norm_back,
            ),
        )
        grad_stream, grad_attn_gain = tied[1]
        grad_tokens = grad_middle + grad_stream

        grad_gate_up = exchange_dp(grad_gate_up, dp_count)
        grad_gate_up = jnp.moveaxis(grad_gate_up.astype(F32), 0, 1)
        grad_gate_w = grad_gate_up[..., :ffn_part].reshape(rows, ffn_width)
        grad_up_w = grad_gate_up[..., ffn_part:].reshape(rows, ffn_width)

        devices = dp_count * seq_shards
        head_gains = jnp.concatenate([grad_qgain, grad_kgain])
        small = jnp.concatenate(
            [
                grad_attn_gain.reshape(devices, rows),
                grad_ffn_gain.reshape(devices, rows),
                jnp.broadcast_to(head_gains, (devices, 2 * head_width)),
            ],
            axis=1,
        )
        small = jnp.sum(lax.all_to_all(small, BOTH, 0, 0, tiled=True), axis=0)
        return (
            output[None],
            grad_tokens[None],
            grad_query_w,
            grad_kv_w[:, :key_width],
            grad_kv_w[:, key_width:],
            grad_out_w,
            small[:rows],
            small[2 * rows : 2 * rows + head_width],
            small[2 * rows + head_width :],
            grad_gate_w,
            grad_up_w,
            grad_down_w.astype(F32),
            small[rows : 2 * rows],
        )

    return body


def solution(mesh):
    in_specs = (
        P("dp", "seq", None),
        P("dp", None),
        P(BOTH, None),
        P(BOTH, None),
        P(BOTH, None),
        P(BOTH, None),
        P(BOTH),
        P(),
        P(),
        P(BOTH, None),
        P(BOTH, None),
        P(BOTH, None),
        P(BOTH),
        P("dp", "seq", None),
    )
    out_specs = (
        P("dp", "seq", None),
        P("dp", "seq", None),
        P(BOTH, None),
        P(BOTH, None),
        P(BOTH, None),
        P(BOTH, None),
        P(BOTH),
        P(),
        P(),
        P(BOTH, None),
        P(BOTH, None),
        P(BOTH, None),
        P(BOTH),
    )
    body = make_body(mesh.shape["dp"], mesh.shape["seq"])
    return jax.shard_map(body, mesh=mesh, in_specs=in_specs, out_specs=out_specs, check_vma=False)
```

```python
import jax
import jax.numpy as jnp
from jax import lax
from jax.sharding import PartitionSpec as P

EPSILON = 1e-05
ROPE_BASE = 1000000.0
F32 = jnp.float32
BF16 = jnp.bfloat16
BOTH = ("dp", "seq")


def rms_scale(values):
    return lax.rsqrt(jnp.mean(values * values, axis=-1, keepdims=True) + EPSILON)


def rope_tables(positions, head_width):
    half_width = head_width // 2
    frequency = ROPE_BASE ** (-(jnp.arange(half_width, dtype=F32) * 2.0 / head_width))
    angles = positions.astype(F32)[:, None] * frequency[None, :]
    return (jnp.cos(angles), jnp.sin(angles))


def rotate(values, cosine_table, sine_table):
    half_width = values.shape[-1] // 2
    front_half = values[..., :half_width]
    back_half = values[..., half_width:]
    return jnp.concatenate(
        [
            front_half * cosine_table - back_half * sine_table,
            back_half * cosine_table + front_half * sine_table,
        ],
        axis=-1,
    )


def unrotate(incoming, cosine_table, sine_table):
    return rotate(incoming, cosine_table, -sine_table)


def norm_back(incoming, values, scale_vec, gain_vector, sum_axes):
    upstream = incoming * gain_vector
    grad_values = scale_vec * (
        upstream
        - values * scale_vec * scale_vec * jnp.mean(upstream * values, axis=-1, keepdims=True)
    )
    grad_gain = jnp.sum(incoming * values * scale_vec, axis=sum_axes)
    return (grad_values, grad_gain)


def dot(left, right):
    return jnp.dot(left, right, preferred_element_type=F32)


def dot_tn(left, right):
    return lax.dot_general(left, right, (((0,), (0,)), ((), ())), preferred_element_type=F32)


def dot_nt(left, right):
    return lax.dot_general(left, right, (((1,), (1,)), ((), ())), preferred_element_type=F32)


def swap_dp(value, bits, count):
    return lax.ppermute(value, "dp", [(i, i ^ bits) for i in range(count)])


def after(value, *others):
    return lax.optimization_barrier((value, *others))[0]


def gather_parts(value, count):
    if count != 4:
        return [lax.all_gather(value, "dp", axis=0, tiled=True)]
    half = value.shape[0] // 2
    one = swap_dp(value, 1, count)
    two = swap_dp(value, 2, count)
    top = swap_dp(two[:half], 1, count)
    bottom = swap_dp(one[half:], 2, count)
    return [value, one, two, jnp.concatenate([top, bottom], axis=0)]


def gather_dp(value, count):
    return jnp.concatenate(gather_parts(value, count), axis=0)


def scatter_steps(parts, count):
    if count != 4:
        return lax.psum_scatter(parts[0], "dp", scatter_dimension=0, tiled=True).astype(F32)
    own, one, two, far = parts
    half = own.shape[0] // 2
    top, bottom = yield (swap_dp(far[:half], 1, count), swap_dp(far[half:], 2, count))
    two_sum = jnp.concatenate(
        [(two[:half].astype(F32) + top.astype(F32)).astype(BF16), two[half:]], axis=0
    )
    one_sum = jnp.concatenate(
        [one[:half], (one[half:].astype(F32) + bottom.astype(F32)).astype(BF16)], axis=0
    )
    from_one, from_two = yield (swap_dp(one_sum, 1, count), swap_dp(two_sum, 2, count))
    return own.astype(F32) + from_one.astype(F32) + from_two.astype(F32)


def run_steps(steps, ties=()):
    tied = []
    ties = list(ties)
    try:
        arrived = next(steps)
        while True:
            if ties:
                held = ties.pop(0)(tied)
                joined = lax.optimization_barrier((*arrived, *held))
                arrived = joined[: len(arrived)]
                tied.append(joined[len(arrived) :])
            arrived = steps.send(tuple(arrived))
    except StopIteration as stop:
        result = stop.value
    for tie in ties:
        tied.append(tuple(tie(tied)))
    return result, tied


def split_rows(value, count):
    if count != 4:
        return [value]
    rows = value.shape[0] // 4
    return [value[i * rows : (i + 1) * rows] for i in range(4)]


def scatter_sum_dp(value, count):
    return run_steps(scatter_steps(split_rows(value, count), count))[0]


def xor_order(value, rank):
    split = value.reshape((2, 2) + value.shape[1:])
    split = jnp.where(rank & 2, split[::-1], split)
    split = jnp.where(rank & 1, split[:, ::-1], split)
    return split.reshape(value.shape)


def exchange_dp(value, count):
    if count != 4:
        return lax.all_to_all(value, "dp", 0, 0, tiled=True)
    rank = lax.axis_index("dp")
    value = xor_order(value, rank)
    value = jnp.stack([value[0]] + [swap_dp(value[j], j, count) for j in range(1, 4)])
    return xor_order(value, rank)


def make_body(dp_count, seq_shards):
    def shift_seq(value, step):
        pairs = [(i, i + step) for i in range(seq_shards) if 0 <= i + step < seq_shards]
        return lax.ppermute(value, "seq", pairs)

    def swap_core(value):
        return lax.ppermute(value, "seq", [(i, i ^ 1) for i in range(seq_shards)])

    def turn_seq(value, step):
        return lax.ppermute(
            value, "seq", [(i, (i + step) % seq_shards) for i in range(seq_shards)]
        )

    pairs = seq_shards // 2
    in_slots = dp_count == 4

    def slot_matrix(width):
        rows = width // (dp_count * seq_shards)
        slot_row = jnp.arange(width, dtype=jnp.int32)
        inner = slot_row % rows
        slot = slot_row // rows
        chip = (lax.axis_index("seq") // 2 + slot % pairs) % pairs
        peer = lax.axis_index("dp") ^ (slot // pairs % dp_count)
        core = (lax.axis_index("seq") % 2) ^ (slot // (pairs * dp_count))
        source = ((peer * seq_shards) + chip * 2 + core) * rows + inner
        return (slot_row[:, None] == source[None, :]).astype(BF16)

    def gather_line(value):
        if not in_slots:
            return value
        line = [value] + [turn_seq(value, -2 * k) for k in range(1, pairs)]
        return jnp.concatenate(line, axis=0)

    def gather_rest(line):
        if not in_slots:
            return lax.all_gather(line, BOTH, axis=0, tiled=True)
        plane = gather_dp(line, dp_count)
        return jnp.concatenate([plane, swap_core(plane)], axis=0)

    def scatter_row_steps(parts):
        if not in_slots:
            return lax.psum_scatter(parts, BOTH, scatter_dimension=0, tiled=True).astype(F32)
        half = parts.shape[0] // 2
        (other,) = yield (swap_core(parts[half:]),)
        chip = (parts[:half].astype(F32) + other.astype(F32)).astype(BF16)
        line = yield from scatter_steps(split_rows(chip, dp_count), dp_count)
        rows = line.shape[0] // pairs
        total = line[:rows]
        for k in range(1, pairs):
            piece = line[k * rows : (k + 1) * rows].astype(BF16)
            total = total + turn_seq(piece, 2 * k).astype(F32)
        return total

    def scatter_rows(parts):
        return run_steps(scatter_row_steps(parts))[0]

    def body(
        tokens,
        segment_ids,
        w_query,
        w_key,
        w_value,
        w_out,
        attn_gain,
        query_gain,
        key_gain,
        w_gate,
        w_up,
        w_down,
        ffn_gain,
        cotangent,
    ):
        _, local_len, model_width = tokens.shape
        seq_len = segment_ids.shape[1]
        head_width = query_gain.shape[0]
        query_width = w_query.shape[1]
        key_width = w_key.shape[1]
        query_heads = query_width // head_width
        key_heads = key_width // head_width
        group_size = query_heads // key_heads
        softmax_scale = head_width ** (-0.5)
        rows = w_query.shape[0]
        ffn_width = w_gate.shape[1]
        ffn_part = ffn_width // dp_count
        seq_rank = lax.axis_index("seq")
        core = seq_rank % 2
        first_row = seq_rank * local_len
        tokens = tokens[0]
        cotangent = cotangent[0]
        ids = segment_ids[0]

        reach = -(-(seq_len // 2 - 1) // local_len)
        hops = -(-reach // 2)

        gains = jnp.stack([attn_gain, ffn_gain], axis=1)
        gains = jnp.pad(gains, ((0, 0), (0, 126)))
        pack_line = gather_line(jnp.concatenate([w_key, w_value, gains], axis=1))
        together = w_out.shape[0] == rows
        first_after = jnp.concatenate([w_query, w_out], axis=1) if together else w_query
        query_line = gather_line(after(first_after, pack_line))
        pack = gather_rest(pack_line)
        kv_all = pack[:, : 2 * key_width]
        gain_cols = pack[:, 2 * key_width :].astype(F32)
        query_all = gather_rest(after(query_line, pack))
        if together:
            query_all, out_all = query_all[:, :query_width], query_all[:, query_width:]
        else:
            out_all = gather_rest(gather_line(after(w_out, query_line)))
        if in_slots:
            slots = slot_matrix(model_width)
            out_slots = slots if query_width == model_width else slot_matrix(query_width)
            to_slots = lambda value, matrix: dot(value, matrix).astype(BF16)
            from_slots = lambda value, matrix: dot_nt(value, matrix).astype(BF16)
            whole_from_slots = lambda value: lax.dot_general(
                value,
                slots.astype(F32),
                (((1,), (1,)), ((), ())),
                precision=lax.Precision.HIGHEST,
                preferred_element_type=F32,
            )
        else:
            slots = out_slots = None
            to_slots = from_slots = lambda value, matrix: value
            whole_from_slots = lambda value: value
        attn_gain_all = gain_cols[:, 0]
        ffn_gain_all = whole_from_slots(gain_cols[:, 1][None])[0]

        gate_up = jnp.concatenate(
            [
                w_gate.reshape(rows, dp_count, ffn_part),
                w_up.reshape(rows, dp_count, ffn_part),
            ],
            axis=2,
        )
        gate_up = exchange_dp(jnp.moveaxis(gate_up, 1, 0), dp_count)
        gate_up = after(gate_up, pack_line)
        down_all = lax.all_gather(after(w_down, gate_up), "seq", axis=0, tiled=True)
        gate_up_all = lax.all_gather(gate_up, "seq", axis=1, tiled=True).reshape(
            model_width, 2 * ffn_part
        )
        cotangent_parts = gather_parts(after(cotangent, pack), dp_count)

        stream = tokens.astype(F32)
        scale_one = rms_scale(stream)
        stream_slots = to_slots(tokens, slots).astype(F32)
        normed_one = (stream_slots * scale_one * attn_gain_all).astype(BF16)
        positions = first_row + jnp.arange(local_len, dtype=jnp.int32)
        cosine_table, sine_table = rope_tables(positions, head_width)
        cosine_table = cosine_table[:, None, :]
        sine_table = sine_table[:, None, :]
        query_pre = dot(normed_one, query_all).reshape(local_len, query_heads, head_width)
        key_value = dot(normed_one, kv_all)
        key_pre = key_value[:, :key_width].reshape(local_len, key_heads, head_width)
        value_send = key_value[:, key_width:].astype(BF16)
        query_scale = rms_scale(query_pre)
        key_scale = rms_scale(key_pre)
        query_gain_f = query_gain.astype(F32)
        key_gain_f = key_gain.astype(F32)
        query_rot = rotate(
            query_pre * query_scale * query_gain_f, cosine_table, sine_table
        ).astype(BF16)
        key_rot = (
            rotate(key_pre * key_scale * key_gain_f, cosine_table, sine_table)
            .astype(BF16)
            .reshape(local_len, key_width)
        )

        both = [jnp.concatenate([key_rot, value_send], axis=1)]
        for _ in range(hops):
            both.append(shift_seq(both[-1], 2))
        for_even = jnp.concatenate(both[:-1], axis=0)
        for_odd = jnp.concatenate(both[1:], axis=0)
        across = swap_core(jnp.where(core == 0, for_even, for_odd))
        window = jnp.concatenate(both + [across], axis=0)
        block_steps = [-2 * i for i in range(hops + 1)] + [-1 - 2 * i for i in range(hops)]
        starts = [first_row + step * local_len for step in block_steps]
        key_pos = jnp.concatenate([start + jnp.arange(local_len, dtype=jnp.int32) for start in starts])
        key_ids = jnp.concatenate(
            [
                lax.dynamic_slice_in_dim(ids, jnp.maximum(start, 0), local_len, 0)
                for start in starts
            ]
        )
        query_ids = lax.dynamic_slice_in_dim(ids, first_row, local_len, 0)
        allowed = (
            (key_pos[None, :] <= positions[:, None])
            & (key_pos[None, :] >= 0)
            & (key_ids[None, :] == query_ids[:, None])
        )[None, None]
        window_len = window.shape[0]
        keys = window[:, :key_width].reshape(window_len, key_heads, head_width)
        values = window[:, key_width:].reshape(window_len, key_heads, head_width)
        queries = query_rot.reshape(local_len, key_heads, group_size, head_width)
        scores = (
            jnp.einsum("qgrd,kgd->grqk", queries, keys, preferred_element_type=F32)
            * softmax_scale
        )
        weights = jnp.where(allowed, jnp.exp(scores), 0.0)
        denominator = jnp.sum(weights, axis=-1)
        summed = jnp.einsum(
            "grqk,kgd->qgrd", weights.astype(BF16), values, preferred_element_type=F32
        )
        attended = (summed / jnp.moveaxis(denominator, 2, 0)[..., None]).astype(BF16)
        log_total = jnp.log(denominator)
        attended_flat = attended.reshape(local_len, query_width)
        attended_slots = to_slots(attended_flat, out_slots)
        middle = stream + dot(attended_slots, out_all)

        scale_two = rms_scale(middle)
        normed_two = (middle * scale_two * ffn_gain_all).astype(BF16)
        def chunked(parts):
            if len(parts) == 1:
                return list(parts)
            own, one, two, far = parts
            return [own, jnp.concatenate([one, two], axis=0), far]

        def parts_of(chunks):
            if len(chunks) == 1:
                return list(chunks)
            own, middle_two, far = chunks
            return [own, middle_two[:local_len], middle_two[local_len:], far]

        def forward(chunk):
            both_pre = dot(chunk, gate_up_all)
            gate_pre = both_pre[:, :ffn_part]
            up_pre = both_pre[:, ffn_part:]
            sigmoid_gate = jax.nn.sigmoid(gate_pre)
            silu_gate = gate_pre * sigmoid_gate
            hidden = (silu_gate * up_pre).astype(BF16)
            return hidden, (gate_pre, up_pre, sigmoid_gate, silu_gate)

        cotangent_chunks = chunked(cotangent_parts)
        if dp_count == 4:
            half = local_len // 2
            one = swap_dp(normed_two, 1, dp_count)
            two = swap_dp(normed_two, 2, dp_count)
            first = forward(normed_two)
            one, two, own_hidden = lax.optimization_barrier((one, two, first[0]))
            top = swap_dp(two[:half], 1, dp_count)
            bottom = swap_dp(one[half:], 2, dp_count)
            near = jnp.concatenate([one, two], axis=0)
            second = forward(near)
            top, bottom, near_hidden = lax.optimization_barrier((top, bottom, second[0]))
            far = jnp.concatenate([top, bottom], axis=0)
            third = forward(far)
            normed_chunks = [normed_two, near, far]
            hidden_chunks = [own_hidden, near_hidden, third[0]]
            saved = [first[1], second[1], third[1]]
        else:
            normed_chunks = [lax.all_gather(normed_two, "dp", axis=0, tiled=True)]
            hidden_all, kept = forward(normed_chunks[0])
            hidden_chunks = [hidden_all]
            saved = [kept]
        def weight_parts(held):
            groups = [held[i : i + chunk_count] for i in range(0, len(held), chunk_count)]
            normed_held, grad_held, hidden_held, cotangent_held = groups
            gate_up_sum = sum(dot_tn(x, y) for x, y in zip(normed_held, grad_held))
            down_sum = sum(dot_tn(x, y) for x, y in zip(hidden_held, cotangent_held))
            return (gate_up_sum.astype(BF16), down_sum.astype(BF16))

        grad_output = cotangent.astype(F32)
        grad_chunks = [None] * len(saved)
        back_chunks = [None] * len(saved)
        previous = None
        for i in reversed(range(len(saved))):
            gate_pre, up_pre, sigmoid_gate, silu_gate = saved[i]
            incoming = cotangent_chunks[i]
            if previous is not None:
                incoming = after(incoming, previous)
            grad_hidden = dot_nt(incoming, down_all)
            grad_gate = (
                grad_hidden * up_pre * sigmoid_gate * (1.0 + gate_pre * (1.0 - sigmoid_gate))
            ).astype(BF16)
            grad_up = (grad_hidden * silu_gate).astype(BF16)
            grad_chunks[i] = jnp.concatenate([grad_gate, grad_up], axis=1)
            back_chunks[i] = dot_nt(grad_chunks[i], gate_up_all).astype(BF16)
            previous = back_chunks[i]
        chunk_count = len(normed_chunks)
        grad_normed_two, tied = run_steps(
            scatter_steps(parts_of(back_chunks), dp_count),
            (
                lambda tied: (*normed_chunks, *grad_chunks, *hidden_chunks, *cotangent_chunks),
                lambda tied: weight_parts(tied[0]),
            ),
        )
        gate_up_part, down_part = tied[1]
        grad_gate_up = lax.psum_scatter(
            gate_up_part.reshape(dp_count, seq_shards * rows, 2 * ffn_part),
            "seq",
            scatter_dimension=1,
            tiled=True,
        )
        grad_down_w = lax.psum_scatter(
            after(down_part, gate_up_part), "seq", scatter_dimension=0, tiled=True
        )
        out_chunks = [dot(chunk, down_all).astype(BF16) for chunk in hidden_chunks]
        output = run_steps(scatter_steps(parts_of(out_chunks), dp_count))[0]
        output = (middle + output).astype(BF16)
        grad_mid_norm, grad_ffn_gain = norm_back(
            grad_normed_two, middle, scale_two, ffn_gain_all, (0,)
        )
        grad_middle = grad_output + grad_mid_norm

        grad_middle_bf = grad_middle.astype(BF16)
        out_steps = scatter_row_steps(dot_tn(attended_slots, grad_middle_bf).astype(BF16))
        grad_attended = from_slots(
            dot_nt(grad_middle_bf, out_all).astype(BF16), out_slots
        ).reshape(local_len, key_heads, group_size, head_width)
        delta_rows = jnp.moveaxis(
            jnp.sum(grad_attended.astype(F32) * attended.astype(F32), axis=-1), 0, 2
        )
        probabilities = jnp.where(allowed, jnp.exp(scores - log_total[..., None]), 0.0)
        grad_probs = jnp.einsum(
            "qgrd,kgd->grqk", grad_attended, values, preferred_element_type=F32
        )
        grad_scores = (probabilities * (grad_probs - delta_rows[..., None])).astype(BF16)
        def query_and_key_term(grad_scores):
            key_term = (
                jnp.einsum("grqk,qgrd->kgd", grad_scores, queries, preferred_element_type=F32)
                * softmax_scale
            )
            grad_query = (
                jnp.einsum("grqk,kgd->qgrd", grad_scores, keys, preferred_element_type=F32)
                * softmax_scale
            )
            return (grad_query, key_term)

        value_term = jnp.einsum(
            "grqk,qgrd->kgd",
            probabilities.astype(BF16),
            grad_attended,
            preferred_element_type=F32,
        )
        grad_out_w, tied = run_steps(
            out_steps,
            (lambda tied: (grad_scores,), lambda tied: query_and_key_term(*tied[0])),
        )
        grad_query, key_term = tied[1]
        grad_window = jnp.concatenate(
            [
                key_term.reshape(window_len, key_width),
                value_term.reshape(window_len, key_width),
            ],
            axis=1,
        ).astype(BF16)
        split = (hops + 1) * local_len
        back = swap_core(grad_window[split:])
        arrived_back = back
        zero = jnp.zeros((local_len, 2 * key_width), BF16)
        back = jnp.where(
            core == 0,
            jnp.concatenate([back, zero], axis=0),
            jnp.concatenate([zero, back], axis=0),
        )
        total = grad_window[:split].astype(F32) + back.astype(F32)
        running = total[hops * local_len :]
        for step in range(hops - 1, -1, -1):
            arrived = shift_seq(running.astype(BF16), -2)
            if step == hops - 1:
                arrived, grad_query = lax.optimization_barrier((arrived, grad_query))
            if step == 0:
                arrived, grad_gate_up = lax.optimization_barrier((arrived, grad_gate_up))
            running = total[step * local_len : (step + 1) * local_len] + arrived.astype(F32)
        key_sum = running[:, :key_width]
        value_grad_bf = running[:, key_width:].astype(BF16)
        grad_qnorm = unrotate(
            grad_query.reshape(local_len, query_heads, head_width), cosine_table, sine_table
        )
        grad_qpre, grad_qgain = norm_back(
            grad_qnorm, query_pre, query_scale, query_gain_f, (0, 1)
        )
        grad_knorm = unrotate(
            key_sum.reshape(local_len, key_heads, head_width), cosine_table, sine_table
        )
        grad_kpre, grad_kgain = norm_back(grad_knorm, key_pre, key_scale, key_gain_f, (0, 1))
        query_bf = grad_qpre.reshape(local_len, query_width).astype(BF16)
        grad_query_w = scatter_rows(
            after(dot_tn(normed_one, query_bf).astype(BF16), arrived_back)
        )
        kv_bf = jnp.concatenate(
            [grad_kpre.reshape(local_len, key_width).astype(BF16), value_grad_bf], axis=1
        )
        kv_part = dot_tn(normed_one, kv_bf).astype(BF16)
        kv_after = after(kv_bf, kv_part)

        def last_norm_back(tied):
            (grad_normed_one,) = tied[0]
            grad_stream, grad_attn_gain = norm_back(
                grad_normed_one, stream_slots, scale_one, attn_gain_all, (0,)
            )
            return (
                whole_from_slots(grad_stream),
                whole_from_slots(grad_attn_gain[None])[0],
            )

        grad_kv_w, tied = run_steps(
            scatter_row_steps(kv_part),
            (
                lambda tied: (dot_nt(query_bf, query_all) + dot_nt(kv_after, kv_all),),
                last_norm_back,
            ),
        )
        grad_stream, grad_attn_gain = tied[1]
        grad_tokens = grad_middle + grad_stream

        grad_gate_up = exchange_dp(grad_gate_up, dp_count)
        grad_gate_up = jnp.moveaxis(grad_gate_up.astype(F32), 0, 1)
        grad_gate_w = grad_gate_up[..., :ffn_part].reshape(rows, ffn_width)
        grad_up_w = grad_gate_up[..., ffn_part:].reshape(rows, ffn_width)

        devices = dp_count * seq_shards
        head_gains = jnp.concatenate([grad_qgain, grad_kgain])
        small = jnp.concatenate(
            [
                grad_attn_gain.reshape(devices, rows),
                grad_ffn_gain.reshape(devices, rows),
                jnp.broadcast_to(head_gains, (devices, 2 * head_width)),
            ],
            axis=1,
        )
        small = jnp.sum(lax.all_to_all(small, BOTH, 0, 0, tiled=True), axis=0)
        return (
            output[None],
            grad_tokens[None],
            grad_query_w,
            grad_kv_w[:, :key_width],
            grad_kv_w[:, key_width:],
            grad_out_w,
            small[:rows],
            small[2 * rows : 2 * rows + head_width],
            small[2 * rows + head_width :],
            grad_gate_w,
            grad_up_w,
            grad_down_w.astype(F32),
            small[rows : 2 * rows],
        )

    return body


def solution(mesh):
    in_specs = (
        P("dp", "seq", None),
        P("dp", None),
        P(BOTH, None),
        P(BOTH, None),
        P(BOTH, None),
        P(BOTH, None),
        P(BOTH),
        P(),
        P(),
        P(BOTH, None),
        P(BOTH, None),
        P(BOTH, None),
        P(BOTH),
        P("dp", "seq", None),
    )
    out_specs = (
        P("dp", "seq", None),
        P("dp", "seq", None),
        P(BOTH, None),
        P(BOTH, None),
        P(BOTH, None),
        P(BOTH, None),
        P(BOTH),
        P(),
        P(),
        P(BOTH, None),
        P(BOTH, None),
        P(BOTH, None),
        P(BOTH),
    )
    body = make_body(mesh.shape["dp"], mesh.shape["seq"])
    return jax.shard_map(body, mesh=mesh, in_specs=in_specs, out_specs=out_specs, check_vma=False)
```

```python
import jax
import jax.numpy as jnp
from jax import lax
from jax.sharding import PartitionSpec as P

EPSILON = 1e-05
ROPE_BASE = 1000000.0
F32 = jnp.float32
BF16 = jnp.bfloat16
BOTH = ("dp", "seq")


def rms_scale(values):
    return lax.rsqrt(jnp.mean(values * values, axis=-1, keepdims=True) + EPSILON)


def rope_tables(positions, head_width):
    half_width = head_width // 2
    frequency = ROPE_BASE ** (-(jnp.arange(half_width, dtype=F32) * 2.0 / head_width))
    angles = positions.astype(F32)[:, None] * frequency[None, :]
    return (jnp.cos(angles), jnp.sin(angles))


def rotate(values, cosine_table, sine_table):
    half_width = values.shape[-1] // 2
    front_half = values[..., :half_width]
    back_half = values[..., half_width:]
    return jnp.concatenate(
        [
            front_half * cosine_table - back_half * sine_table,
            back_half * cosine_table + front_half * sine_table,
        ],
        axis=-1,
    )


def unrotate(incoming, cosine_table, sine_table):
    return rotate(incoming, cosine_table, -sine_table)


def norm_back(incoming, values, scale_vec, gain_vector, sum_axes):
    upstream = incoming * gain_vector
    grad_values = scale_vec * (
        upstream
        - values * scale_vec * scale_vec * jnp.mean(upstream * values, axis=-1, keepdims=True)
    )
    grad_gain = jnp.sum(incoming * values * scale_vec, axis=sum_axes)
    return (grad_values, grad_gain)


def dot(left, right):
    return jnp.dot(left, right, preferred_element_type=F32)


def dot_tn(left, right):
    return lax.dot_general(left, right, (((0,), (0,)), ((), ())), preferred_element_type=F32)


def dot_nt(left, right):
    return lax.dot_general(left, right, (((1,), (1,)), ((), ())), preferred_element_type=F32)


def swap_dp(value, bits, count):
    return lax.ppermute(value, "dp", [(i, i ^ bits) for i in range(count)])


def after(value, *others):
    return lax.optimization_barrier((value, *others))[0]


def gather_parts(value, count):
    if count != 4:
        return [lax.all_gather(value, "dp", axis=0, tiled=True)]
    half = value.shape[0] // 2
    one = swap_dp(value, 1, count)
    two = swap_dp(value, 2, count)
    top = swap_dp(two[:half], 1, count)
    bottom = swap_dp(one[half:], 2, count)
    return [value, one, two, jnp.concatenate([top, bottom], axis=0)]


def gather_dp(value, count):
    return jnp.concatenate(gather_parts(value, count), axis=0)


def scatter_steps(parts, count):
    if count != 4:
        return lax.psum_scatter(parts[0], "dp", scatter_dimension=0, tiled=True).astype(F32)
    own, one, two, far = parts
    half = own.shape[0] // 2
    top, bottom = yield (swap_dp(far[:half], 1, count), swap_dp(far[half:], 2, count))
    two_sum = jnp.concatenate(
        [(two[:half].astype(F32) + top.astype(F32)).astype(BF16), two[half:]], axis=0
    )
    one_sum = jnp.concatenate(
        [one[:half], (one[half:].astype(F32) + bottom.astype(F32)).astype(BF16)], axis=0
    )
    from_one, from_two = yield (swap_dp(one_sum, 1, count), swap_dp(two_sum, 2, count))
    return own.astype(F32) + from_one.astype(F32) + from_two.astype(F32)


def run_steps(steps, ties=()):
    tied = []
    ties = list(ties)
    try:
        arrived = next(steps)
        while True:
            if ties:
                held = ties.pop(0)(tied)
                joined = lax.optimization_barrier((*arrived, *held))
                arrived = joined[: len(arrived)]
                tied.append(joined[len(arrived) :])
            arrived = steps.send(tuple(arrived))
    except StopIteration as stop:
        result = stop.value
    for tie in ties:
        tied.append(tuple(tie(tied)))
    return result, tied


def split_rows(value, count):
    if count != 4:
        return [value]
    rows = value.shape[0] // 4
    return [value[i * rows : (i + 1) * rows] for i in range(4)]


def scatter_sum_dp(value, count):
    return run_steps(scatter_steps(split_rows(value, count), count))[0]


def xor_order(value, rank):
    split = value.reshape((2, 2) + value.shape[1:])
    split = jnp.where(rank & 2, split[::-1], split)
    split = jnp.where(rank & 1, split[:, ::-1], split)
    return split.reshape(value.shape)


def exchange_dp(value, count):
    if count != 4:
        return lax.all_to_all(value, "dp", 0, 0, tiled=True)
    rank = lax.axis_index("dp")
    value = xor_order(value, rank)
    value = jnp.stack([value[0]] + [swap_dp(value[j], j, count) for j in range(1, 4)])
    return xor_order(value, rank)


def make_body(dp_count, seq_shards):
    def shift_seq(value, step):
        pairs = [(i, i + step) for i in range(seq_shards) if 0 <= i + step < seq_shards]
        return lax.ppermute(value, "seq", pairs)

    def swap_core(value):
        return lax.ppermute(value, "seq", [(i, i ^ 1) for i in range(seq_shards)])

    def turn_seq(value, step):
        return lax.ppermute(
            value, "seq", [(i, (i + step) % seq_shards) for i in range(seq_shards)]
        )

    pairs = seq_shards // 2
    in_slots = dp_count == 4

    def slot_matrix(width):
        rows = width // (dp_count * seq_shards)
        slot_row = jnp.arange(width, dtype=jnp.int32)
        inner = slot_row % rows
        slot = slot_row // rows
        chip = (lax.axis_index("seq") // 2 + slot % pairs) % pairs
        peer = lax.axis_index("dp") ^ (slot // pairs % dp_count)
        core = (lax.axis_index("seq") % 2) ^ (slot // (pairs * dp_count))
        source = ((peer * seq_shards) + chip * 2 + core) * rows + inner
        return (slot_row[:, None] == source[None, :]).astype(BF16)

    def gather_line(value):
        if not in_slots:
            return value
        line = [value] + [turn_seq(value, -2 * k) for k in range(1, pairs)]
        return jnp.concatenate(line, axis=0)

    def gather_rest(line):
        if not in_slots:
            return lax.all_gather(line, BOTH, axis=0, tiled=True)
        plane = gather_dp(line, dp_count)
        return jnp.concatenate([plane, swap_core(plane)], axis=0)

    def scatter_row_steps(parts):
        if not in_slots:
            return lax.psum_scatter(parts, BOTH, scatter_dimension=0, tiled=True).astype(F32)
        half = parts.shape[0] // 2
        (other,) = yield (swap_core(parts[half:]),)
        chip = (parts[:half].astype(F32) + other.astype(F32)).astype(BF16)
        line = yield from scatter_steps(split_rows(chip, dp_count), dp_count)
        rows = line.shape[0] // pairs
        total = line[:rows]
        for k in range(1, pairs):
            piece = line[k * rows : (k + 1) * rows].astype(BF16)
            total = total + turn_seq(piece, 2 * k).astype(F32)
        return total

    def scatter_rows(parts):
        return run_steps(scatter_row_steps(parts))[0]

    def body(
        tokens,
        segment_ids,
        w_query,
        w_key,
        w_value,
        w_out,
        attn_gain,
        query_gain,
        key_gain,
        w_gate,
        w_up,
        w_down,
        ffn_gain,
        cotangent,
    ):
        _, local_len, model_width = tokens.shape
        seq_len = segment_ids.shape[1]
        head_width = query_gain.shape[0]
        query_width = w_query.shape[1]
        key_width = w_key.shape[1]
        query_heads = query_width // head_width
        key_heads = key_width // head_width
        group_size = query_heads // key_heads
        softmax_scale = head_width ** (-0.5)
        rows = w_query.shape[0]
        ffn_width = w_gate.shape[1]
        ffn_part = ffn_width // dp_count
        seq_rank = lax.axis_index("seq")
        core = seq_rank % 2
        first_row = seq_rank * local_len
        tokens = tokens[0]
        cotangent = cotangent[0]
        ids = segment_ids[0]

        reach = -(-(seq_len // 2 - 1) // local_len)
        hops = -(-reach // 2)

        gains = jnp.stack([attn_gain, ffn_gain], axis=1)
        gains = jnp.pad(gains, ((0, 0), (0, 126)))
        pack_line = gather_line(jnp.concatenate([w_key, w_value, gains], axis=1))
        together = w_out.shape[0] == rows
        first_after = jnp.concatenate([w_query, w_out], axis=1) if together else w_query
        query_line = gather_line(after(first_after, pack_line))
        pack = gather_rest(pack_line)
        kv_all = pack[:, : 2 * key_width]
        gain_cols = pack[:, 2 * key_width :].astype(F32)
        query_all = gather_rest(after(query_line, pack))
        if together:
            query_all, out_all = query_all[:, :query_width], query_all[:, query_width:]
        else:
            out_all = gather_rest(gather_line(after(w_out, query_line)))
        if in_slots:
            slots = slot_matrix(model_width)
            out_slots = slots if query_width == model_width else slot_matrix(query_width)
            to_slots = lambda value, matrix: dot(value, matrix).astype(BF16)
            from_slots = lambda value, matrix: dot_nt(value, matrix).astype(BF16)
            whole_from_slots = lambda value: lax.dot_general(
                value,
                slots.astype(F32),
                (((1,), (1,)), ((), ())),
                precision=lax.Precision.HIGHEST,
                preferred_element_type=F32,
            )
        else:
            slots = out_slots = None
            to_slots = from_slots = lambda value, matrix: value
            whole_from_slots = lambda value: value
        attn_gain_all = gain_cols[:, 0]
        ffn_gain_all = whole_from_slots(gain_cols[:, 1][None])[0]

        gate_up = jnp.concatenate(
            [
                w_gate.reshape(rows, dp_count, ffn_part),
                w_up.reshape(rows, dp_count, ffn_part),
            ],
            axis=2,
        )
        gate_up = exchange_dp(jnp.moveaxis(gate_up, 1, 0), dp_count)
        gate_up = after(gate_up, pack_line)
        down_all = lax.all_gather(after(w_down, gate_up), "seq", axis=0, tiled=True)
        gate_up_all = lax.all_gather(gate_up, "seq", axis=1, tiled=True).reshape(
            model_width, 2 * ffn_part
        )
        cotangent_parts = gather_parts(after(cotangent, pack), dp_count)

        stream = tokens.astype(F32)
        scale_one = rms_scale(stream)
        stream_slots = to_slots(tokens, slots).astype(F32)
        normed_one = (stream_slots * scale_one * attn_gain_all).astype(BF16)
        positions = first_row + jnp.arange(local_len, dtype=jnp.int32)
        cosine_table, sine_table = rope_tables(positions, head_width)
        cosine_table = cosine_table[:, None, :]
        sine_table = sine_table[:, None, :]
        query_pre = dot(normed_one, query_all).reshape(local_len, query_heads, head_width)
        key_value = dot(normed_one, kv_all)
        key_pre = key_value[:, :key_width].reshape(local_len, key_heads, head_width)
        value_send = key_value[:, key_width:].astype(BF16)
        query_scale = rms_scale(query_pre)
        key_scale = rms_scale(key_pre)
        query_gain_f = query_gain.astype(F32)
        key_gain_f = key_gain.astype(F32)
        query_rot = rotate(
            query_pre * query_scale * query_gain_f, cosine_table, sine_table
        ).astype(BF16)
        key_rot = (
            rotate(key_pre * key_scale * key_gain_f, cosine_table, sine_table)
            .astype(BF16)
            .reshape(local_len, key_width)
        )

        both = [jnp.concatenate([key_rot, value_send], axis=1)]
        for _ in range(hops):
            both.append(shift_seq(both[-1], 2))
        for_even = jnp.concatenate(both[:-1], axis=0)
        for_odd = jnp.concatenate(both[1:], axis=0)
        across = swap_core(jnp.where(core == 0, for_even, for_odd))
        window = jnp.concatenate(both + [across], axis=0)
        block_steps = [-2 * i for i in range(hops + 1)] + [-1 - 2 * i for i in range(hops)]
        starts = [first_row + step * local_len for step in block_steps]
        key_pos = jnp.concatenate([start + jnp.arange(local_len, dtype=jnp.int32) for start in starts])
        key_ids = jnp.concatenate(
            [
                lax.dynamic_slice_in_dim(ids, jnp.maximum(start, 0), local_len, 0)
                for start in starts
            ]
        )
        query_ids = lax.dynamic_slice_in_dim(ids, first_row, local_len, 0)
        allowed = (
            (key_pos[None, :] <= positions[:, None])
            & (key_pos[None, :] >= 0)
            & (key_ids[None, :] == query_ids[:, None])
        )[None, None]
        window_len = window.shape[0]
        keys = window[:, :key_width].reshape(window_len, key_heads, head_width)
        values = window[:, key_width:].reshape(window_len, key_heads, head_width)
        queries = query_rot.reshape(local_len, key_heads, group_size, head_width)
        scores = (
            jnp.einsum("qgrd,kgd->grqk", queries, keys, preferred_element_type=F32)
            * softmax_scale
        )
        weights = jnp.where(allowed, jnp.exp(scores), 0.0)
        denominator = jnp.sum(weights, axis=-1)
        summed = jnp.einsum(
            "grqk,kgd->qgrd", weights.astype(BF16), values, preferred_element_type=F32
        )
        attended = (summed / jnp.moveaxis(denominator, 2, 0)[..., None]).astype(BF16)
        log_total = jnp.log(denominator)
        attended_flat = attended.reshape(local_len, query_width)
        attended_slots = to_slots(attended_flat, out_slots)
        middle = stream + dot(attended_slots, out_all)

        scale_two = rms_scale(middle)
        normed_two = (middle * scale_two * ffn_gain_all).astype(BF16)
        def chunked(parts):
            if len(parts) == 1:
                return list(parts)
            own, one, two, far = parts
            return [own, jnp.concatenate([one, two], axis=0), far]

        def parts_of(chunks):
            if len(chunks) == 1:
                return list(chunks)
            own, middle_two, far = chunks
            return [own, middle_two[:local_len], middle_two[local_len:], far]

        def forward(chunk):
            both_pre = dot(chunk, gate_up_all)
            gate_pre = both_pre[:, :ffn_part]
            up_pre = both_pre[:, ffn_part:]
            sigmoid_gate = jax.nn.sigmoid(gate_pre)
            silu_gate = gate_pre * sigmoid_gate
            hidden = (silu_gate * up_pre).astype(BF16)
            return hidden, (gate_pre, up_pre, sigmoid_gate, silu_gate)

        cotangent_chunks = chunked(cotangent_parts)
        if dp_count == 4:
            half = local_len // 2
            one = swap_dp(normed_two, 1, dp_count)
            two = swap_dp(normed_two, 2, dp_count)
            first = forward(normed_two)
            one, two, own_hidden = lax.optimization_barrier((one, two, first[0]))
            top = swap_dp(two[:half], 1, dp_count)
            bottom = swap_dp(one[half:], 2, dp_count)
            near = jnp.concatenate([one, two], axis=0)
            second = forward(near)
            top, bottom, near_hidden = lax.optimization_barrier((top, bottom, second[0]))
            far = jnp.concatenate([top, bottom], axis=0)
            third = forward(far)
            normed_chunks = [normed_two, near, far]
            hidden_chunks = [own_hidden, near_hidden, third[0]]
            saved = [first[1], second[1], third[1]]
        else:
            normed_chunks = [lax.all_gather(normed_two, "dp", axis=0, tiled=True)]
            hidden_all, kept = forward(normed_chunks[0])
            hidden_chunks = [hidden_all]
            saved = [kept]
        def weight_parts(held):
            groups = [held[i : i + chunk_count] for i in range(0, len(held), chunk_count)]
            normed_held, grad_held, hidden_held, cotangent_held = groups
            gate_up_sum = sum(dot_tn(x, y) for x, y in zip(normed_held, grad_held))
            down_sum = sum(dot_tn(x, y) for x, y in zip(hidden_held, cotangent_held))
            return (gate_up_sum.astype(BF16), down_sum.astype(BF16))

        grad_output = cotangent.astype(F32)
        grad_chunks = [None] * len(saved)
        back_chunks = [None] * len(saved)
        previous = None
        for i in reversed(range(len(saved))):
            gate_pre, up_pre, sigmoid_gate, silu_gate = saved[i]
            incoming = cotangent_chunks[i]
            if previous is not None:
                incoming = after(incoming, previous)
            grad_hidden = dot_nt(incoming, down_all)
            grad_gate = (
                grad_hidden * up_pre * sigmoid_gate * (1.0 + gate_pre * (1.0 - sigmoid_gate))
            ).astype(BF16)
            grad_up = (grad_hidden * silu_gate).astype(BF16)
            grad_chunks[i] = jnp.concatenate([grad_gate, grad_up], axis=1)
            back_chunks[i] = dot_nt(grad_chunks[i], gate_up_all).astype(BF16)
            previous = back_chunks[i]
        chunk_count = len(normed_chunks)
        grad_normed_two, tied = run_steps(
            scatter_steps(parts_of(back_chunks), dp_count),
            (
                lambda tied: (*normed_chunks, *grad_chunks, *hidden_chunks, *cotangent_chunks),
                lambda tied: weight_parts(tied[0]),
            ),
        )
        gate_up_part, down_part = tied[1]
        grad_gate_up = lax.psum_scatter(
            gate_up_part.reshape(dp_count, seq_shards * rows, 2 * ffn_part),
            "seq",
            scatter_dimension=1,
            tiled=True,
        )
        grad_down_w = lax.psum_scatter(
            after(down_part, gate_up_part), "seq", scatter_dimension=0, tiled=True
        )
        out_chunks = [dot(chunk, down_all).astype(BF16) for chunk in hidden_chunks]
        output = run_steps(scatter_steps(parts_of(out_chunks), dp_count))[0]
        output = (middle + output).astype(BF16)
        grad_mid_norm, grad_ffn_gain = norm_back(
            grad_normed_two, middle, scale_two, ffn_gain_all, (0,)
        )
        grad_middle = grad_output + grad_mid_norm

        grad_middle_bf = grad_middle.astype(BF16)
        out_steps = scatter_row_steps(dot_tn(attended_slots, grad_middle_bf).astype(BF16))
        grad_attended = from_slots(
            dot_nt(grad_middle_bf, out_all).astype(BF16), out_slots
        ).reshape(local_len, key_heads, group_size, head_width)
        delta_rows = jnp.moveaxis(
            jnp.sum(grad_attended.astype(F32) * attended.astype(F32), axis=-1), 0, 2
        )
        probabilities = jnp.where(allowed, jnp.exp(scores - log_total[..., None]), 0.0)
        grad_probs = jnp.einsum(
            "qgrd,kgd->grqk", grad_attended, values, preferred_element_type=F32
        )
        grad_scores = (probabilities * (grad_probs - delta_rows[..., None])).astype(BF16)
        def query_and_key_term(grad_scores):
            key_term = (
                jnp.einsum("grqk,qgrd->kgd", grad_scores, queries, preferred_element_type=F32)
                * softmax_scale
            )
            grad_query = (
                jnp.einsum("grqk,kgd->qgrd", grad_scores, keys, preferred_element_type=F32)
                * softmax_scale
            )
            return (grad_query, key_term)

        value_term = jnp.einsum(
            "grqk,qgrd->kgd",
            probabilities.astype(BF16),
            grad_attended,
            preferred_element_type=F32,
        )
        grad_out_w, tied = run_steps(
            out_steps,
            (lambda tied: (grad_scores,), lambda tied: query_and_key_term(*tied[0])),
        )
        grad_query, key_term = tied[1]
        grad_window = jnp.concatenate(
            [
                key_term.reshape(window_len, key_width),
                value_term.reshape(window_len, key_width),
            ],
            axis=1,
        ).astype(BF16)
        split = (hops + 1) * local_len
        back = swap_core(grad_window[split:])
        zero = jnp.zeros((local_len, 2 * key_width), BF16)
        back = jnp.where(
            core == 0,
            jnp.concatenate([back, zero], axis=0),
            jnp.concatenate([zero, back], axis=0),
        )
        total = grad_window[:split].astype(F32) + back.astype(F32)
        running = total[hops * local_len :]
        for step in range(hops - 1, 0, -1):
            arrived = shift_seq(running.astype(BF16), -2)
            if step == hops - 1:
                arrived, grad_query = lax.optimization_barrier((arrived, grad_query))
            running = total[step * local_len : (step + 1) * local_len] + arrived.astype(F32)
        arrived = shift_seq(running.astype(BF16), -2)
        grad_qnorm = unrotate(
            grad_query.reshape(local_len, query_heads, head_width), cosine_table, sine_table
        )
        grad_qpre, grad_qgain = norm_back(
            grad_qnorm, query_pre, query_scale, query_gain_f, (0, 1)
        )
        query_bf = grad_qpre.reshape(local_len, query_width).astype(BF16)
        grad_query_w, tied = run_steps(
            scatter_row_steps(dot_tn(normed_one, query_bf).astype(BF16)),
            (lambda tied, held=(arrived, grad_gate_up): held,),
        )
        arrived, grad_gate_up = tied[0]
        running = total[:local_len] + arrived.astype(F32)
        key_sum = running[:, :key_width]
        value_grad_bf = running[:, key_width:].astype(BF16)
        grad_knorm = unrotate(
            key_sum.reshape(local_len, key_heads, head_width), cosine_table, sine_table
        )
        grad_kpre, grad_kgain = norm_back(grad_knorm, key_pre, key_scale, key_gain_f, (0, 1))
        kv_bf = jnp.concatenate(
            [grad_kpre.reshape(local_len, key_width).astype(BF16), value_grad_bf], axis=1
        )
        kv_part = dot_tn(normed_one, kv_bf).astype(BF16)
        kv_after = after(kv_bf, kv_part)

        def last_norm_back(tied):
            (grad_normed_one,) = tied[0]
            grad_stream, grad_attn_gain = norm_back(
                grad_normed_one, stream_slots, scale_one, attn_gain_all, (0,)
            )
            return (
                whole_from_slots(grad_stream),
                whole_from_slots(grad_attn_gain[None])[0],
            )

        grad_kv_w, tied = run_steps(
            scatter_row_steps(kv_part),
            (
                lambda tied: (dot_nt(query_bf, query_all) + dot_nt(kv_after, kv_all),),
                last_norm_back,
            ),
        )
        grad_stream, grad_attn_gain = tied[1]
        grad_tokens = grad_middle + grad_stream

        grad_gate_up = exchange_dp(grad_gate_up, dp_count)
        grad_gate_up = jnp.moveaxis(grad_gate_up.astype(F32), 0, 1)
        grad_gate_w = grad_gate_up[..., :ffn_part].reshape(rows, ffn_width)
        grad_up_w = grad_gate_up[..., ffn_part:].reshape(rows, ffn_width)

        devices = dp_count * seq_shards
        head_gains = jnp.concatenate([grad_qgain, grad_kgain])
        small = jnp.concatenate(
            [
                grad_attn_gain.reshape(devices, rows),
                grad_ffn_gain.reshape(devices, rows),
                jnp.broadcast_to(head_gains, (devices, 2 * head_width)),
            ],
            axis=1,
        )
        small = jnp.sum(lax.all_to_all(small, BOTH, 0, 0, tiled=True), axis=0)
        return (
            output[None],
            grad_tokens[None],
            grad_query_w,
            grad_kv_w[:, :key_width],
            grad_kv_w[:, key_width:],
            grad_out_w,
            small[:rows],
            small[2 * rows : 2 * rows + head_width],
            small[2 * rows + head_width :],
            grad_gate_w,
            grad_up_w,
            grad_down_w.astype(F32),
            small[rows : 2 * rows],
        )

    return body


def solution(mesh):
    in_specs = (
        P("dp", "seq", None),
        P("dp", None),
        P(BOTH, None),
        P(BOTH, None),
        P(BOTH, None),
        P(BOTH, None),
        P(BOTH),
        P(),
        P(),
        P(BOTH, None),
        P(BOTH, None),
        P(BOTH, None),
        P(BOTH),
        P("dp", "seq", None),
    )
    out_specs = (
        P("dp", "seq", None),
        P("dp", "seq", None),
        P(BOTH, None),
        P(BOTH, None),
        P(BOTH, None),
        P(BOTH, None),
        P(BOTH),
        P(),
        P(),
        P(BOTH, None),
        P(BOTH, None),
        P(BOTH, None),
        P(BOTH),
    )
    body = make_body(mesh.shape["dp"], mesh.shape["seq"])
    return jax.shard_map(body, mesh=mesh, in_specs=in_specs, out_specs=out_specs, check_vma=False)
```
